32 devices in a mesh: group: 2 (over x), ccd: 16 (over z, y, core).
Axes of the slice: x: 2, y: 2, z: 4, core: 2. Of those that a mesh axis runs over, the one named last changes fastest.
Arguments:
- images: float32 [4, 4096, 512], P(None, ('group', 'ccd')), parts along dimension 1, may hold values from -6 to 6
- basis_taps: float32 [2, 9, 11], replicated, may hold values from -1.75 to 1.75
- psf_coef: float32 [4, 10, 9, 3], P(None, 'group'), parts along dimension 1, may hold values from -3 to 3
- affine: float32 [4, 10, 2, 2], P(None, 'group'), parts along dimension 1, may hold values from -0.5 to 0.5
- visit_weight: bfloat16 [4, 10], P(None, 'group'), parts along dimension 1, may hold values from 0.25 to 4
- block_patch: int32 [32, 16, 1], P(('group', 'ccd')), parts along dimension 0, may hold values from 0 to 15; in each aligned block of 16 rows (0 to 15, 16 to 31, ..., all dimensions but the last counted through in order) at most 2 rows name the same one
- block_slot: int32 [32, 16], P(('group', 'ccd')), parts along dimension 0, may hold values from 0 to 15
- patch_owner: int32 [32], P('group'), parts along dimension 0, may hold values from 0 to 15, each once
Outputs:
- coadd: float32 [32, 512, 512], P(('group', 'ccd')), parts along dimension 0
The draws below stay inside these ranges and needn't reach their ends.
There are 2 independent parts, one for each index of `group`. The reference program is written for one: setup_inputs(seed, part) draws one part's arguments, and reference() takes and returns one part's arrays. A program takes and returns all parts, laid end to end along the dimension named above; an argument that names none is the same for every part. Nothing has to cross between parts.
Inputs may be any that keep to these rules, and one draw needn't show every extreme that they name: `block_patch`: among the 16 blocks of one band no patch is named more than 2 times, and in every draw some band names some patch exactly 2 times. `patch_owner`: each device index along ccd owns exactly one patch.
All inputs are finite; a program needn't handle non-finite values.
Results may differ from the reference program's by a relative error of at most 0.0029.
Values may be sent and summed in bfloat16 or wider, within the bound.
A program may use at most 64 MiB of HBM per device.

```python
import math
import jax
import jax.numpy as jnp
import numpy as np
from jax import lax

V = 4
BLOCK = 128
BLKC = 4
SPLIT = 4
TAPS = 11
NBASIS = 9
PSIDE = 4
BANDS = 16
NCCD = 5
NPATCH = 16
BLK_DEV = 16
CAP = 2


def touch_ends(result, own_key, low, high):
    place = [jax.random.randint(jax.random.fold_in(own_key, axis), (), 0, length) for axis, length in enumerate(result.shape)]
    longest = result.shape.index(max(result.shape))
    beside = place[:longest] + [(place[longest] + 1) % result.shape[longest]] + place[longest + 1:]
    return result.at[tuple(place)].set(low).at[tuple(beside)].set(high)


def level_of(own_key, extent, pieces, low, largest):
    def one(axis_at, parts):
        draws = jax.random.uniform(jax.random.fold_in(jax.random.fold_in(own_key, 6), axis_at), (parts,), jnp.float32, low / len(pieces), largest / len(pieces))
        return jnp.repeat(jnp.exp(draws), extent[axis_at] // parts).reshape((-1,) + (1,) * (len(extent) - axis_at - 1))

    level = one(*pieces[0])
    for cut in pieces[1:]:
        level = level * one(*cut)
    return level


def shared_out(rng, own, number, rows, amount, top, limit, lean):
    ranking = jax.random.permutation(rng, amount)
    crowded, usual = shares(amount, rows * top, limit, lean, True), shares(amount, rows * top, limit, lean, False)
    places = jnp.arange(amount)

    def named(lengths, offset_by):
        used = int((lengths > 0).sum())
        fixed = max(1, used // 4)
        passed = fixed + (places - fixed + offset_by * (used - fixed)) % max(1, amount - fixed)
        return jnp.zeros((amount,), jnp.int32).at[ranking[jnp.where(places < fixed, places, passed)]].set(jnp.asarray(lengths, jnp.int32))

    lengths = jnp.where(number % 4 == 0, named(crowded, number // 4), named(usual, number - number // 4 - 1))
    mixed = jax.random.permutation(jax.random.fold_in(own, 3), amount)
    source_of, taker = mixed[0:amount // 2 * 2:2], mixed[1:amount // 2 * 2:2]
    margin = jnp.minimum(lengths[source_of] - 1, limit - lengths[taker]) // 2
    margin = jnp.where((source_of == ranking[0]) | (taker == ranking[0]) | (lengths[taker] == 0), 0, jnp.maximum(margin, 0))
    passed = jax.random.randint(jax.random.fold_in(own, 4), (amount // 2,), 0, 1 << 20) % (margin + 1)
    lengths = lengths.at[source_of].add(-passed).at[taker].add(passed)
    labels = jnp.searchsorted(jnp.cumsum(lengths), jnp.arange(rows * top), side="right").astype(jnp.int32)
    listing = labels.reshape(top, rows).T
    listing = listing[jax.random.permutation(jax.random.fold_in(own, 1), rows)]
    offset_by = jax.random.randint(jax.random.fold_in(own, 2), (rows, 1), 0, top)
    return jnp.take_along_axis(listing, (jnp.arange(top)[None, :] + offset_by) % top, axis=1)


def shares(count, total, most, slope, full):
    weights = [(1 << 20) // math.isqrt(grade ** slope) + 1 for grade in range(1, count + 1)]
    largest = most if full else min(most, max(-(-total // count), total * weights[0] // sum(weights)))
    least = 1 if total - largest >= count - 1 else 0
    given, surplus = [largest] + [least] * (count - 1), total - largest - least * (count - 1)
    while surplus > 0:
        candidates = [i for i in range(1, count) if given[i] < largest] or [i for i in range(1, count) if given[i] < most]
        pool, left = sum([weights[i] for i in candidates]), surplus
        for i in candidates:
            more = min(most - given[i], max(1, left * weights[i] // pool), surplus)
            given[i] = given[i] + more
            surplus = surplus - more
    return np.array(given)


def bell_draw(rng, shape, spread, most, cuts=(), kind=jnp.bfloat16):
    values = spread * jax.random.normal(rng, shape, jnp.float32)
    if cuts:
        values = values * level_of(rng, shape, cuts, -0.22, 0.18)
    return jnp.clip(values, -most, most).astype(kind)


def setup_inputs(seed: int = 0, part: int = 0) -> dict:
    splits = jax.random.split(jax.random.key(seed), 9)
    part_splits = jax.random.split(jax.random.fold_in(splits[8], part), 9)
    images = bell_draw(part_splits[0], (V, BANDS * BLOCK, BLKC * BLOCK), 1.0, 6.0, ((1, 16),), jnp.float32)
    basis_taps = bell_draw(splits[1], (2, NBASIS, TAPS), TAPS ** -0.5, 1.75, (), jnp.float32)
    psf_coef = bell_draw(part_splits[2], (V, NCCD, NBASIS, 3), 0.35, 3.0, (), jnp.float32)
    affine = jnp.clip(jax.random.uniform(part_splits[3], (V, NCCD, 2, 2), jnp.float32, -0.5, 0.5), -0.5, 0.5)
    visit_weight = jnp.clip(jnp.exp(jax.random.uniform(part_splits[4], (V, NCCD), jnp.float32, math.log(0.25), math.log(4.0))), 0.25, 4.0).astype(jnp.bfloat16)
    block_patch_keys = jax.random.split(jax.random.fold_in(part_splits[5], 1), BANDS * BLK_DEV // BLK_DEV)
    block_patch_turns = jax.random.permutation(jax.random.fold_in(part_splits[5], 3), BANDS * BLK_DEV // BLK_DEV)
    block_patch = jax.vmap(lambda own, number: shared_out(jax.random.fold_in(part_splits[5], 2), own, number, BLK_DEV, NPATCH, 1, CAP, 2))(block_patch_keys, block_patch_turns).reshape((BANDS, BLK_DEV, 1))
    block_slot = touch_ends(jax.random.randint(part_splits[6], (BANDS, BLK_DEV), 0, PSIDE * PSIDE), jax.random.fold_in(part_splits[6], 1), 0, (PSIDE * PSIDE) - 1).astype(jnp.int32)
    patch_owner = jax.random.permutation(part_splits[7], NPATCH).astype(jnp.int32)
    return {"images": images, "basis_taps": basis_taps, "psf_coef": psf_coef, "affine": affine, "visit_weight": visit_weight, "block_patch": block_patch, "block_slot": block_slot, "patch_owner": patch_owner}


def lanczos(offset):
    inside = jnp.abs(offset) < 3.0
    return jnp.where(inside, jnp.sinc(offset) * jnp.sinc(offset / 3.0), 0.0)


def match_warp(inputs, basis_taps):
    ccd_image, psf_terms, affine_map, ccd_number = inputs
    height = SPLIT * BLOCK
    ccd_width = BLKC * BLOCK
    half_taps = TAPS // 2
    offset_rows = (SPLIT // 2) * BLOCK
    row_pos = (2.0 * jnp.arange(height, dtype=jnp.float32) + 1.0) / height - 1.0
    col_pos = (2.0 * jnp.arange(ccd_width, dtype=jnp.float32) + 1.0) / ccd_width - 1.0
    padded = jnp.pad(ccd_image, ((0, 0), (half_taps, half_taps)))
    matched = jnp.zeros((height, ccd_width), jnp.float32)
    for basis_index in range(NBASIS):
        column_pass = jnp.zeros((height, ccd_width), jnp.float32)
        for tap_index in range(TAPS):
            column_pass = column_pass + basis_taps[1, basis_index, tap_index] * padded[:, tap_index:tap_index + ccd_width]
        row_padded = jnp.pad(column_pass, ((half_taps, half_taps), (0, 0)))
        row_pass = jnp.zeros((height, ccd_width), jnp.float32)
        for tap_index in range(TAPS):
            row_pass = row_pass + basis_taps[0, basis_index, tap_index] * row_padded[tap_index:tap_index + height]
        spatial = psf_terms[basis_index, 0] + psf_terms[basis_index, 1] * row_pos[:, None] + psf_terms[basis_index, 2] * col_pos[None, :]
        matched = matched + spatial * row_pass
    region_row = ccd_number * height + jnp.arange(height, dtype=jnp.int32) - offset_rows
    keep = ((region_row >= 0) & (region_row < BANDS * BLOCK)).astype(jnp.float32)
    matched = matched * keep[:, None]
    rows_global = jnp.arange(height, dtype=jnp.float32)
    row_shift = affine_map[0, 0] + affine_map[0, 1] * (rows_global - (height - 1) / 2.0) / height
    framed = jnp.pad(matched, ((3, 3), (0, 0)))
    row_warped = jnp.zeros((height, ccd_width), jnp.float32)
    for step_index in range(-3, 4):
        row_warped = row_warped + lanczos(row_shift - step_index)[:, None] * framed[3 + step_index:3 + step_index + height]
    cols_global = jnp.arange(ccd_width, dtype=jnp.float32)
    col_shift = affine_map[1, 0] + affine_map[1, 1] * (cols_global - (ccd_width - 1) / 2.0) / ccd_width
    framed_cols = jnp.pad(row_warped, ((0, 0), (3, 3)))
    warped = jnp.zeros((height, ccd_width), jnp.float32)
    for step_index in range(-3, 4):
        warped = warped + lanczos(col_shift - step_index)[None, :] * framed_cols[:, 3 + step_index:3 + step_index + ccd_width]
    return warped.astype(jnp.bfloat16)


def reference(images, basis_taps, psf_coef, affine, visit_weight, block_patch, block_slot, patch_owner):
    height = SPLIT * BLOCK
    ccd_width = BLKC * BLOCK
    offset_rows = (SPLIT // 2) * BLOCK
    tail_rows = NCCD * height - BANDS * BLOCK - offset_rows
    padded_images = jnp.pad(images, ((0, 0), (offset_rows, tail_rows), (0, 0)))
    stacked = padded_images.reshape(V * NCCD, height, ccd_width)
    psf_terms = psf_coef.reshape(V * NCCD, NBASIS, 3)
    affine_maps = affine.reshape(V * NCCD, 2, 2)
    ccd_numbers = jnp.tile(jnp.arange(NCCD, dtype=jnp.int32), V)

    def one_ccd(inputs):
        return match_warp(inputs, basis_taps)

    warped = lax.map(one_ccd, (stacked, psf_terms, affine_maps, ccd_numbers))
    warped = warped.reshape(V, NCCD * height, ccd_width)[:, offset_rows:offset_rows + BANDS * BLOCK]
    blocks = warped.reshape(V, BANDS, BLOCK, BLKC, BLOCK).transpose(1, 0, 3, 2, 4)
    blocks = blocks.reshape(BANDS * V * BLKC, BLOCK * BLOCK)
    band_ccd = (jnp.arange(BANDS, dtype=jnp.int32) + SPLIT // 2) // SPLIT
    weights = visit_weight.astype(jnp.float32).T[band_ccd]
    weights = jnp.repeat(weights, BLKC, axis=1).reshape(-1)
    cells = PSIDE * PSIDE
    segment_ids = (block_patch[:, :, 0] * cells + block_slot).reshape(-1).astype(jnp.int32)
    contrib = weights[:, None] * blocks.astype(jnp.float32)
    numerator = jax.ops.segment_sum(contrib, segment_ids, num_segments=NPATCH * cells)
    denominator = jax.ops.segment_sum(weights, segment_ids, num_segments=NPATCH * cells)
    patches = numerator / jnp.maximum(denominator, 1.0)[:, None]
    patches = patches.reshape(NPATCH, PSIDE, PSIDE, BLOCK, BLOCK).transpose(0, 1, 3, 2, 4)
    patches = patches.reshape(NPATCH, PSIDE * BLOCK, PSIDE * BLOCK)
    coadd = jnp.zeros_like(patches).at[patch_owner].set(patches)
    return coadd
```

```python
import functools
import math

import jax
import jax.numpy as jnp
from jax import lax
from jax.experimental import pallas as pl
from jax.experimental.pallas import tpu as pltpu
from jax.sharding import PartitionSpec as P

V = 4
BLOCK = 128
BLKC = 4
SPLIT = 4
TAPS = 11
NBASIS = 9
PSIDE = 4
CELLS = PSIDE * PSIDE
HALF = TAPS // 2
REACH = 3
RIM = HALF + REACH
CHUNK = 32
ORDER = (1, 2, 0, 3)
EXT = BLOCK + 2 * RIM
ROWS_IN = CHUNK + 2 * RIM
ROWS_MID = CHUNK + 8
WIDTH = BLKC * BLOCK
HEIGHT = SPLIT * BLOCK
LEFT = BLOCK // 2
STEPS = 2 * REACH + 1
COUNT = V * BLKC
DEPTH = NBASIS * ROWS_IN
FRESH = {1: (32, 48), 2: (80, 32), 0: (0, 32), 3: (112, 32)}
SINE = [(-1) ** k * math.pi ** (2 * k + 1) / math.factorial(2 * k + 1) for k in range(7)]


def sin_pi(values):
    whole = jnp.floor(values + 0.5)
    rest = values - whole
    odd = whole - 2.0 * jnp.floor(whole * 0.5)
    square = rest * rest
    total = jnp.full(values.shape, SINE[-1], jnp.float32)
    for factor in SINE[-2::-1]:
        total = total * square + factor
    return total * rest * (1.0 - 2.0 * odd)


def lanczos(offset):
    near = jnp.abs(offset) < 1e-4
    safe = jnp.where(near, 1.0, offset)
    value = sin_pi(safe) * sin_pi(safe / 3.0) * (3.0 / math.pi**2) / (safe * safe)
    value = jnp.where(near, 1.0, value)
    return jnp.where(jnp.abs(offset) < 3.0, value, 0.0)


def outward(count):
    far = sorted(range(1, count), key=lambda step: abs(step - count // 2))
    half = len(far) // 2
    near = far[half:][::-1]
    mixed = [step for pair in zip(far[:half], near) for step in pair]
    return mixed + near[half:]


def split(values):
    high = values.astype(jnp.bfloat16)
    return high, (values - high.astype(jnp.float32)).astype(jnp.bfloat16)


def dot(left, right):
    return jnp.dot(left, right, preferred_element_type=jnp.float32)


def band_kernel(
    devices,
    capacity,
    taps_ref,
    coef_ref,
    affine_ref,
    patch_ref,
    slot_ref,
    owner_ref,
    weight_ref,
    image_ref,
    table_ref,
    got_ref,
    ext,
    col_kernel,
    row_kernel,
    lhs,
    terms_high,
    terms_low,
    row_weight,
    col_weight,
    mid,
    stage,
    outbox,
    notes,
    plan,
    sent,
    received,
    own,
    rims,
):
    band = lax.axis_index("ccd")
    barrier = pltpu.get_barrier_semaphore()
    chunks = len(ORDER)
    for step in range(1, devices):
        pl.semaphore_signal(
            barrier,
            inc=1,
            device_id={"ccd": lax.rem(band + step, devices)},
            device_id_type=pl.DeviceIdType.MESH,
        )
    load = pltpu.make_async_copy(image_ref, ext.at[:, pl.ds(RIM, BLOCK)], own.at[chunks + 1])
    load.start()

    shifted = band + SPLIT // 2
    ccd = shifted // SPLIT
    top_row = shifted % SPLIT * BLOCK
    region_shift = band * BLOCK - top_row
    region_low = jnp.maximum(0, -region_shift)
    region_high = jnp.minimum(HEIGHT, devices * BLOCK - region_shift)

    def inside(first, count):
        rows = first + lax.broadcasted_iota(jnp.int32, (count, 1), 0)
        return (rows >= region_low) & (rows < region_high)

    owners = [owner_ref[patch_ref[block]] for block in range(COUNT)]
    lane_row = lax.broadcasted_iota(jnp.int32, (1, BLOCK), 1)
    weight_lane = lax.broadcasted_iota(jnp.int32, weight_ref.shape, 1)
    weights = jnp.sum(
        jnp.where(weight_lane == ccd, weight_ref[...].astype(jnp.float32), 0.0), axis=1, keepdims=True
    )

    def plan_one(device, carry):
        first, last = jnp.int32(COUNT), jnp.int32(-1)
        for block in range(COUNT):
            mine = owners[block] == device
            first = jnp.where(mine & (first == COUNT), block, first)
            last = jnp.where(mine, block, last)
        some = last >= 0
        first = jnp.where(some, first, 0)
        two = some & (last != first)
        last = jnp.where(some, last, 0)
        plan[device * capacity] = first
        plan[device * capacity + 1] = last
        for slot in range(2, capacity):
            plan[device * capacity + slot] = 0
        note = jnp.where(lane_row == 0, slot_ref[0, first], jnp.where(lane_row == 1, slot_ref[0, last], 0))
        note = note.astype(jnp.float32)
        for visit in range(V):
            here = jnp.broadcast_to(weights[visit : visit + 1], (1, BLOCK))
            pick_first = (lane_row == 2) & (some & (first // BLKC == visit))
            pick_last = (lane_row == 3) & (two & (last // BLKC == visit))
            note = jnp.where(pick_first | pick_last, here, note)
        notes[device] = note
        return carry

    lax.fori_loop(0, devices, plan_one, 0)

    low_row, high_row = LEFT - HALF - LEFT % 8 - 3, 200
    low_row = low_row // 16 * 16
    high_row = -(-(LEFT + HALF + BLOCK) // 16) * 16
    spread = high_row - low_row
    distance = (
        low_row
        + lax.broadcasted_iota(jnp.int32, (spread, BLOCK), 0)
        - lax.broadcasted_iota(jnp.int32, (spread, BLOCK), 1)
        - (LEFT - HALF)
    )
    col_kernel[...] = jnp.zeros_like(col_kernel)

    def col_one(basis, carry):
        total = jnp.zeros((spread, BLOCK), jnp.float32)
        for tap in range(TAPS):
            total = jnp.where(distance == tap, taps_ref[basis, 1, tap], total)
        high, low = split(total)
        cols = pl.ds(pl.multiple_of(basis * BLOCK, BLOCK), BLOCK)
        col_kernel[pl.ds(low_row, spread), cols] = high
        col_kernel[pl.ds(2 * BLOCK + low_row, spread), cols] = high
        col_kernel[pl.ds(4 * BLOCK + low_row, spread), cols] = low
        return carry

    lax.fori_loop(0, NBASIS, col_one, 0)

    wide_lane = lax.broadcasted_iota(jnp.int32, (1, DEPTH), 1)
    starts = [wide_lane >= basis * ROWS_IN for basis in range(NBASIS)]

    def by_basis(value):
        total = jnp.full((1, DEPTH), value(0), jnp.float32)
        for basis in range(1, NBASIS):
            total = jnp.where(starts[basis], value(basis), total)
        return total

    start = jnp.zeros((1, DEPTH), jnp.int32)
    for basis in range(1, NBASIS):
        start = jnp.where(starts[basis], basis * ROWS_IN, start)
    gap = (wide_lane - start) - lax.broadcasted_iota(jnp.int32, (ROWS_MID, DEPTH), 0)
    total = jnp.zeros(gap.shape, jnp.float32)
    for tap in range(TAPS):
        total = jnp.where(gap == tap, by_basis(lambda basis: taps_ref[basis, 0, tap]), total)
    row_kernel[...] = total

    lane = lax.broadcasted_iota(jnp.int32, (1, BLOCK), 1)
    base, slope = jnp.zeros((1, BLOCK), jnp.float32), jnp.zeros((1, BLOCK), jnp.float32)
    for visit in range(V):
        base = jnp.where(lane // 8 == visit, affine_ref[visit, 0, 0, ccd], base)
        slope = jnp.where(lane // 8 == visit, affine_ref[visit, 0, 1, ccd], slope)
    own_rows = (top_row + lax.broadcasted_iota(jnp.int32, (BLOCK, BLOCK), 0)).astype(jnp.float32)
    row_shift = base + slope * ((own_rows - (HEIGHT - 1) / 2.0) / HEIGHT)
    row_step = (lane % 8 - REACH).astype(jnp.float32)
    all_rows = lanczos(row_shift - row_step)
    column = lax.broadcasted_iota(jnp.int32, (1, WIDTH), 1).astype(jnp.float32)
    col_pos = (2.0 * column + 1.0) / WIDTH - 1.0
    col_step = lax.broadcasted_iota(jnp.int32, (8, WIDTH), 0) - REACH
    reached = lax.broadcasted_iota(jnp.int32, (8, WIDTH), 1) + col_step
    for visit in range(V):
        row_weight[visit] = all_rows if visit == 0 else pltpu.roll(all_rows, BLOCK - 8 * visit, 1)
        col_shift = affine_ref[visit, 1, 0, ccd] + affine_ref[visit, 1, 1, ccd] * (
            (column - (WIDTH - 1) / 2.0) / WIDTH
        )
        col_weight[visit] = jnp.where(
            (reached >= 0) & (reached < WIDTH), lanczos(col_shift - col_step.astype(jnp.float32)), 0.0
        )

    def remote(source, target, kind, step):
        return pltpu.make_async_remote_copy(
            src_ref=source,
            dst_ref=target,
            send_sem=sent.at[kind, step],
            recv_sem=received.at[kind, step],
            device_id={"ccd": lax.rem(band + step, devices)},
            device_id_type=pl.DeviceIdType.MESH,
        )

    has_next, has_last = band < devices - 1, band > 0

    def to_next():
        return pltpu.make_async_remote_copy(
            src_ref=image_ref.at[:, pl.ds(BLOCK - RIM, RIM)],
            dst_ref=ext.at[:, pl.ds(0, RIM)],
            send_sem=rims.at[0],
            recv_sem=rims.at[1],
            device_id={"ccd": lax.rem(band + 1, devices)},
            device_id_type=pl.DeviceIdType.MESH,
        )

    def to_last():
        return pltpu.make_async_remote_copy(
            src_ref=image_ref.at[:, pl.ds(0, RIM)],
            dst_ref=ext.at[:, pl.ds(RIM + BLOCK, RIM)],
            send_sem=rims.at[2],
            recv_sem=rims.at[3],
            device_id={"ccd": lax.rem(band + devices - 1, devices)},
            device_id_type=pl.DeviceIdType.MESH,
        )

    load.wait()
    waits = []
    for turn, chunk in enumerate(ORDER):
        if chunk == 0:
            @pl.when(has_next)
            def _():
                to_next().wait_send()
                to_last().wait_recv()

            @pl.when(has_last)
            def _():
                to_last().wait_send()
                to_next().wait_recv()

        fresh, fresh_rows = FRESH[chunk]
        for visit in range(V):
            raw = ext[visit, fresh : fresh + fresh_rows]
            raw = jnp.where(inside(top_row + fresh - RIM, fresh_rows), raw, 0.0)
            side = jnp.zeros((fresh_rows, LEFT), jnp.bfloat16)
            high, low = (jnp.concatenate([side, part, side], axis=1) for part in split(raw))
            for block in range(BLKC):
                rows = pl.ds((block * V + visit) * fresh_rows, fresh_rows)
                window = slice(block * BLOCK, (block + 2) * BLOCK)
                lhs[rows, 0 : 2 * BLOCK] = high[:, window]
                lhs[rows, 2 * BLOCK : 4 * BLOCK] = low[:, window]
        done = COUNT * fresh_rows
        for basis in range(NBASIS):
            cols = pl.ds(basis * BLOCK, BLOCK)
            left = jnp.concatenate([lhs[0:done, :], lhs[0:done, 0 : 2 * BLOCK]], axis=1)
            high, low = split(dot(left, col_kernel[:, cols]))
            for block in range(BLKC):
                for visit in range(V):
                    rows = slice((block * V + visit) * fresh_rows, (block * V + visit + 1) * fresh_rows)
                    into = pl.ds(fresh, fresh_rows), pl.ds(block * BLOCK, BLOCK)
                    terms_high[visit, basis, into[0], into[1]] = high[rows]
                    terms_low[visit, basis, into[0], into[1]] = low[rows]

        first = top_row + chunk * CHUNK

        def one_visit(visit, carry, chunk=chunk, first=first):
            position = (first - REACH + lax.broadcasted_iota(jnp.int32, (ROWS_MID, 1), 0)).astype(
                jnp.float32
            )
            row_pos = (2.0 * position + 1.0) / HEIGHT - 1.0
            kernel = row_kernel[...]
            constant, by_row, by_column = (
                by_basis(lambda basis: coef_ref[ccd, part, visit, basis]) for part in range(3)
            )
            level = kernel * (constant + by_row * row_pos)
            high, low = split(jnp.concatenate([level, kernel * by_column], axis=0))
            rows = pl.ds(chunk * CHUNK, ROWS_IN)
            upper = dot(
                jnp.concatenate([high, low], axis=0), terms_high[visit, :, rows, :].reshape(DEPTH, WIDTH)
            )
            lower = dot(high, terms_low[visit, :, rows, :].reshape(DEPTH, WIDTH))
            both = upper[: 2 * ROWS_MID] + upper[2 * ROWS_MID :] + lower
            matched = both[:ROWS_MID] + both[ROWS_MID:] * col_pos
            mid[...] = jnp.where(inside(first - REACH, ROWS_MID), matched, 0.0)

            weight = row_weight[visit, pl.ds(chunk * CHUNK, CHUNK)]
            warped = jnp.zeros((CHUNK, WIDTH), jnp.float32)
            for step in range(STEPS):
                warped = warped + weight[:, step : step + 1] * mid[step : step + CHUNK, :]
            weight = col_weight[visit]
            total = jnp.zeros((CHUNK, WIDTH), jnp.float32)
            for step in range(STEPS):
                offset = step - REACH
                moved = warped if offset == 0 else pltpu.roll(warped, (-offset) % WIDTH, 1)
                total = total + weight[step : step + 1, :] * moved
            rounded = total.astype(jnp.bfloat16)
            for block in range(BLKC):
                stage[turn % 2, visit * BLKC + block] = rounded[:, block * BLOCK : (block + 1) * BLOCK]
            return carry

        lax.fori_loop(0, V, one_visit, 0)
        rows = pl.ds(chunk * CHUNK, CHUNK)
        for device in range(devices):
            for slot in range(capacity):
                outbox[device, slot, rows] = stage[turn % 2, plan[device * capacity + slot]]
        if turn == 0:
            pl.semaphore_wait(barrier, devices - 1)

            @pl.when(has_next)
            def _():
                to_next().start()

            @pl.when(has_last)
            def _():
                to_last().start()

        batch = []
        for step in outward(devices):
            target = lax.rem(band + step, devices)
            batch.append(
                remote(outbox.at[target, :, rows], got_ref.at[band, :, rows], chunk, step)
            )
        batch.append(
            pltpu.make_async_copy(outbox.at[band, :, rows], got_ref.at[band, :, rows], own.at[chunk])
        )
        if turn == 0:
            for step in outward(devices):
                batch.append(
                    remote(notes.at[lax.rem(band + step, devices)], table_ref.at[band], chunks, step)
                )
            batch.append(pltpu.make_async_copy(notes.at[band], table_ref.at[band], own.at[chunks]))
        for copy in batch:
            copy.start()
        waits += batch
    for copy in waits:
        copy.wait()


def gather_kernel(devices, capacity, table_ref, got_ref, out_ref, blocks, total, weights, sems):
    loads = [
        pltpu.make_async_copy(got_ref.at[source], blocks.at[source], sems.at[source])
        for source in range(devices)
    ]
    for load in loads:
        load.start()
    total[...] = jnp.zeros_like(total)
    for cell in range(CELLS):
        weights[cell] = 0.0
    for load in loads:
        load.wait()

    def add(source, carry):
        for slot in range(2):
            weight = table_ref[source, 0, 2 + slot]

            @pl.when(weight > 0.0)
            def _():
                cell = table_ref[source, 0, slot].astype(jnp.int32)
                weights[cell] = weights[cell] + weight
                total[cell] = total[cell] + weight * blocks[source, slot].astype(jnp.float32)

        return carry

    lax.fori_loop(0, devices, add, 0)
    for cell in range(CELLS):
        row, col = cell // PSIDE * BLOCK, cell % PSIDE * BLOCK
        scale = 1.0 / jnp.full((1, BLOCK), jnp.maximum(weights[cell], 1.0), jnp.float32)
        out_ref[0, row : row + BLOCK, col : col + BLOCK] = total[cell] * scale


def shards(
    images, basis_taps, psf_coef, affine, visit_weight, block_patch, block_slot, patch_owner
):
    devices = lax.axis_size("ccd")
    capacity = max(2, (2 * COUNT + devices - 1) // devices)
    anywhere = pl.BlockSpec(memory_space=pl.ANY)
    scalars = pl.BlockSpec(memory_space=pltpu.SMEM)
    vector = pl.BlockSpec(memory_space=pltpu.VMEM)
    chunks = len(ORDER)
    half = jnp.bfloat16
    table, got = pl.pallas_call(
        functools.partial(band_kernel, devices, capacity),
        out_shape=(
            jax.ShapeDtypeStruct((devices, 1, BLOCK), jnp.float32),
            jax.ShapeDtypeStruct((devices, capacity, BLOCK, BLOCK), half),
        ),
        in_specs=[scalars] * 6 + [vector, anywhere],
        out_specs=(vector, anywhere),
        scratch_shapes=[
            pltpu.VMEM((V, EXT, WIDTH), jnp.float32),
            pltpu.VMEM((6 * BLOCK, NBASIS * BLOCK), half),
            pltpu.VMEM((ROWS_MID, DEPTH), jnp.float32),
            pltpu.VMEM((COUNT * ROWS_IN, 4 * BLOCK), half),
            pltpu.VMEM((V, NBASIS, EXT, WIDTH), half),
            pltpu.VMEM((V, NBASIS, EXT, WIDTH), half),
            pltpu.VMEM((V, BLOCK, BLOCK), jnp.float32),
            pltpu.VMEM((V, 8, WIDTH), jnp.float32),
            pltpu.VMEM((ROWS_MID, WIDTH), jnp.float32),
            pltpu.VMEM((2, COUNT, CHUNK, BLOCK), half),
            pltpu.VMEM((devices, capacity, BLOCK, BLOCK), half),
            pltpu.VMEM((devices, 1, BLOCK), jnp.float32),
            pltpu.SMEM((devices * capacity,), jnp.int32),
            pltpu.SemaphoreType.DMA((chunks + 1, devices)),
            pltpu.SemaphoreType.DMA((chunks + 1, devices)),
            pltpu.SemaphoreType.DMA((chunks + 2,)),
            pltpu.SemaphoreType.DMA((4,)),
        ],
        compiler_params=pltpu.CompilerParams(collective_id=1, has_side_effects=True),
    )(
        basis_taps.transpose(1, 0, 2),
        psf_coef.transpose(1, 3, 0, 2),
        affine.transpose(0, 2, 3, 1),
        block_patch.reshape(-1),
        block_slot,
        patch_owner,
        visit_weight,
        images,
    )
    size = PSIDE * BLOCK
    return pl.pallas_call(
        functools.partial(gather_kernel, devices, capacity),
        out_shape=jax.ShapeDtypeStruct((1, size, size), jnp.float32),
        in_specs=[scalars, anywhere],
        out_specs=vector,
        scratch_shapes=[
            pltpu.VMEM((devices, capacity, BLOCK, BLOCK), half),
            pltpu.VMEM((CELLS, BLOCK, BLOCK), jnp.float32),
            pltpu.SMEM((CELLS,), jnp.float32),
            pltpu.SemaphoreType.DMA((devices,)),
        ],
    )(table, got)


def solution(mesh):
    placed = (
        P(None, ("group", "ccd"), None),
        P(),
        P(None, "group", None, None),
        P(None, "group", None, None),
        P(None, "group"),
        P(("group", "ccd"), None, None),
        P(("group", "ccd"), None),
        P("group"),
    )
    return jax.shard_map(
        shards,
        mesh=mesh,
        in_specs=placed,
        out_specs=P(("group", "ccd"), None, None),
        check_vma=False,
    )
```

```python
import functools
import math

import jax
import jax.numpy as jnp
from jax import lax
from jax.experimental import pallas as pl
from jax.experimental.pallas import tpu as pltpu
from jax.sharding import PartitionSpec as P

V = 4
BLOCK = 128
BLKC = 4
SPLIT = 4
TAPS = 11
NBASIS = 9
PSIDE = 4
CELLS = PSIDE * PSIDE
HALF = TAPS // 2
REACH = 3
RIM = HALF + REACH
CHUNK = 32
CAP = 2
GROUP = 16
EXT = BLOCK + 2 * RIM
ROWS_IN = CHUNK + 2 * RIM
ROWS_MID = CHUNK + 8
WIDTH = BLKC * BLOCK
HEIGHT = SPLIT * BLOCK
LEFT = 16
WINDOW = BLOCK + 2 * LEFT
STEPS = 2 * REACH + 1
COUNT = V * BLKC
DEPTH = NBASIS * ROWS_IN
ORDER = (1, 2, 0, 3)
FRESH = ((32, 48), (80, 32), (0, 32), (112, 32))
SENDS = ((0,), (1,), (2, 3))
SINE = [(-1) ** k * math.pi ** (2 * k + 1) / math.factorial(2 * k + 1) for k in range(7)]


def sin_pi(values):
    whole = jnp.floor(values + 0.5)
    rest = values - whole
    odd = whole - 2.0 * jnp.floor(whole * 0.5)
    square = rest * rest
    total = jnp.full(values.shape, SINE[-1], jnp.float32)
    for factor in SINE[-2::-1]:
        total = total * square + factor
    return total * rest * (1.0 - 2.0 * odd)


def finish(product, offset):
    near = jnp.abs(offset) < 1e-4
    square = jnp.where(near, 1.0, offset * offset)
    value = jnp.where(near, 1.0, product * (3.0 / math.pi**2) / square)
    return jnp.where(jnp.abs(offset) < 3.0, value, 0.0)


def lanczos(offset):
    return finish(sin_pi(offset) * sin_pi(offset / 3.0), offset)


def outward(count):
    far = sorted(range(1, count), key=lambda step: abs(step - count // 2))
    half = len(far) // 2
    near = far[half:][::-1]
    mixed = [step for pair in zip(far[:half], near) for step in pair]
    return mixed + near[half:]


def split(values):
    high = values.astype(jnp.bfloat16)
    return high, (values - high.astype(jnp.float32)).astype(jnp.bfloat16)


def dot(left, right):
    return jnp.dot(left, right, preferred_element_type=jnp.float32)


def band_kernel(
    devices,
    taps_ref,
    coef_ref,
    affine_ref,
    patch_ref,
    slot_ref,
    owner_ref,
    weight_ref,
    image_ref,
    out_ref,
    ext,
    col_kernel,
    lhs,
    terms_high,
    terms_low,
    mid,
    stage,
    outbox,
    inbox,
    notes,
    table,
    picks,
    plan,
    sent,
    received,
    own,
    rims,
):
    band = lax.axis_index("ccd")
    barrier = pltpu.get_barrier_semaphore()
    sends = len(SENDS)
    for step in range(1, devices):
        pl.semaphore_signal(
            barrier,
            inc=1,
            device_id={"ccd": lax.rem(band + step, devices)},
            device_id_type=pl.DeviceIdType.MESH,
        )
    load = pltpu.make_async_copy(image_ref, ext.at[:, pl.ds(RIM, BLOCK)], own.at[sends + 1])
    load.start()

    shifted = band + SPLIT // 2
    ccd = shifted // SPLIT
    top_row = shifted % SPLIT * BLOCK
    region_shift = band * BLOCK - top_row
    region_low = jnp.maximum(0, -region_shift)
    region_high = jnp.minimum(HEIGHT, devices * BLOCK - region_shift)
    lane = lax.broadcasted_iota(jnp.int32, (1, BLOCK), 1)

    def inside(first, count):
        rows = first + lax.broadcasted_iota(jnp.int32, (count, 1), 0)
        return (rows >= region_low) & (rows < region_high)

    weight_lane = lax.broadcasted_iota(jnp.int32, weight_ref.shape, 1)
    weights = jnp.sum(
        jnp.where(weight_lane == ccd, weight_ref[...].astype(jnp.float32), 0.0), axis=1, keepdims=True
    )
    owners = jnp.full((1, BLOCK), -1, jnp.int32)
    cells = jnp.zeros((1, BLOCK), jnp.float32)
    block_weight = jnp.zeros((1, BLOCK), jnp.float32)
    for block in range(COUNT):
        owners = jnp.where(lane == block, owner_ref[patch_ref[block]], owners)
        cells = jnp.where(lane == block, slot_ref[0, block].astype(jnp.float32), cells)
    for visit in range(V):
        here = jnp.broadcast_to(weights[visit : visit + 1], (1, BLOCK))
        block_weight = jnp.where(lane // BLKC == visit, here, block_weight)
    lanes = lax.broadcasted_iota(jnp.int32, (devices, BLOCK), 1)
    match = owners == lax.broadcasted_iota(jnp.int32, (devices, BLOCK), 0)
    first = jnp.min(jnp.where(match, lanes, BLOCK), axis=1, keepdims=True)
    last = jnp.max(jnp.where(match, lanes, -1), axis=1, keepdims=True)
    is_first, is_last = lanes == first, lanes == last

    def at(chosen, values):
        return jnp.sum(jnp.where(chosen, values, 0.0), axis=1, keepdims=True)

    note = jnp.where(
        lanes < 2 * GROUP,
        jnp.where(lanes < GROUP, at(is_first, cells), at(is_last, cells)),
        jnp.where(
            lanes < 3 * GROUP, at(is_first, block_weight), at(is_last & (last > first), block_weight)
        ),
    )
    picks[...] = jnp.where(lanes == 0, jnp.where(last < 0, 0, first), jnp.maximum(last, 0))
    to_plan = pltpu.make_async_copy(picks, plan, own.at[sends + 2])
    to_plan.start()
    for device in range(devices):
        notes[device] = note[device : device + 1]

    sub = lax.broadcasted_iota(jnp.int32, (8, BLOCK), 0)
    across = lax.broadcasted_iota(jnp.int32, (8, BLOCK), 1)
    edge = LEFT - HALF
    for basis in range(NBASIS):
        taps = jnp.zeros((8, BLOCK), jnp.float32)
        for tap in range(TAPS):
            taps = jnp.where(across == BLOCK - edge - tap, taps_ref[basis, 1, tap], taps)
        taps = pltpu.roll(taps, 0, 1, stride=1, stride_axis=0)
        high = taps.astype(jnp.bfloat16).astype(jnp.float32)
        low = taps - high
        cols = slice(basis * BLOCK, (basis + 1) * BLOCK)
        for part, offsets in ((high, (0, WINDOW)), (low, (2 * WINDOW,))):
            rows = []
            for group in range(WINDOW // 8):
                turned = pltpu.roll(part, group * 8 % BLOCK, 1) if group * 8 % BLOCK else part
                tap = group * 8 + sub - edge - across
                rows.append(jnp.where((tap >= 0) & (tap < TAPS), turned, 0.0))
            matrix = jnp.concatenate(rows, axis=0).astype(jnp.bfloat16)
            for offset in offsets:
                col_kernel[offset : offset + WINDOW, cols] = matrix

    wide_lane = lax.broadcasted_iota(jnp.int32, (1, DEPTH), 1)
    starts = [wide_lane >= basis * ROWS_IN for basis in range(NBASIS)]

    def by_basis(value):
        total = jnp.full((1, DEPTH), value(0), jnp.float32)
        for basis in range(1, NBASIS):
            total = jnp.where(starts[basis], value(basis), total)
        return total

    start = jnp.zeros((1, DEPTH), jnp.int32)
    for basis in range(1, NBASIS):
        start = jnp.where(starts[basis], basis * ROWS_IN, start)
    gap = (wide_lane - start) - lax.broadcasted_iota(jnp.int32, (ROWS_MID, DEPTH), 0)
    row_kernel = jnp.zeros(gap.shape, jnp.float32)
    for tap in range(TAPS):
        row_kernel = jnp.where(gap == tap, by_basis(lambda basis: taps_ref[basis, 0, tap]), row_kernel)

    column = lax.broadcasted_iota(jnp.int32, (1, WIDTH), 1).astype(jnp.float32)
    col_pos = (2.0 * column + 1.0) / WIDTH - 1.0
    line = lax.broadcasted_iota(jnp.int32, (8, 1), 0)
    base, slope = jnp.zeros((8, 1), jnp.float32), jnp.zeros((8, 1), jnp.float32)
    for visit in range(V):
        base = jnp.where(line == visit, affine_ref[visit, 1, 0, ccd], base)
        slope = jnp.where(line == visit, affine_ref[visit, 1, 1, ccd], slope)
    col_shift = base + slope * ((column - (WIDTH - 1) / 2.0) / WIDTH)
    sine = sin_pi(col_shift)
    third_sine, third_cosine = sin_pi(col_shift / 3.0), sin_pi(col_shift / 3.0 + 0.5)
    turn_cos, turn_sin = jnp.zeros((8, 1), jnp.float32), jnp.zeros((8, 1), jnp.float32)
    for step in range(STEPS):
        k = step - REACH
        turn_cos = jnp.where(line == step, (-1) ** k * math.cos(math.pi * k / 3), turn_cos)
        turn_sin = jnp.where(line == step, (-1) ** k * math.sin(math.pi * k / 3), turn_sin)
    col_step = lax.broadcasted_iota(jnp.int32, (8, WIDTH), 0) - REACH
    reached = lax.broadcasted_iota(jnp.int32, (8, WIDTH), 1) + col_step
    reached = (reached >= 0) & (reached < WIDTH)
    col_weight = []
    for visit in range(V):
        row = slice(visit, visit + 1)
        product = sine[row] * (third_sine[row] * turn_cos - third_cosine[row] * turn_sin)
        weight = finish(product, col_shift[row] - col_step.astype(jnp.float32))
        col_weight.append(jnp.where(reached, weight, 0.0))

    row_base, row_slope = jnp.zeros((1, BLOCK), jnp.float32), jnp.zeros((1, BLOCK), jnp.float32)
    for visit in range(V):
        row_base = jnp.where(lane // 8 == visit, affine_ref[visit, 0, 0, ccd], row_base)
        row_slope = jnp.where(lane // 8 == visit, affine_ref[visit, 0, 1, ccd], row_slope)
    row_step = (lane % 8 - REACH).astype(jnp.float32)

    def remote(source, target, kind, step):
        return pltpu.make_async_remote_copy(
            src_ref=source,
            dst_ref=target,
            send_sem=sent.at[kind, step],
            recv_sem=received.at[kind, step],
            device_id={"ccd": lax.rem(band + step, devices)},
            device_id_type=pl.DeviceIdType.MESH,
        )

    has_next, has_last = band < devices - 1, band > 0

    def to_next():
        return pltpu.make_async_remote_copy(
            src_ref=image_ref.at[:, pl.ds(BLOCK - RIM, RIM)],
            dst_ref=ext.at[:, pl.ds(0, RIM)],
            send_sem=rims.at[0],
            recv_sem=rims.at[1],
            device_id={"ccd": lax.rem(band + 1, devices)},
            device_id_type=pl.DeviceIdType.MESH,
        )

    def to_last():
        return pltpu.make_async_remote_copy(
            src_ref=image_ref.at[:, pl.ds(0, RIM)],
            dst_ref=ext.at[:, pl.ds(RIM + BLOCK, RIM)],
            send_sem=rims.at[2],
            recv_sem=rims.at[3],
            device_id={"ccd": lax.rem(band + devices - 1, devices)},
            device_id_type=pl.DeviceIdType.MESH,
        )

    load.wait()
    batches = []
    for turn, chunk in enumerate(ORDER):
        if chunk == 0:
            @pl.when(has_next)
            def _():
                to_next().wait_send()
                to_last().wait_recv()

            @pl.when(has_last)
            def _():
                to_last().wait_send()
                to_next().wait_recv()

        fresh, count = FRESH[turn]
        for visit in range(V):
            raw = ext[visit, fresh : fresh + count]
            raw = jnp.where(inside(top_row + fresh - RIM, count), raw, 0.0)
            side = jnp.zeros((count, LEFT), jnp.bfloat16)
            high, low = (jnp.concatenate([side, part, side], axis=1) for part in split(raw))
            for block in range(BLKC):
                rows = slice((block * V + visit) * count, (block * V + visit + 1) * count)
                window = slice(block * BLOCK, block * BLOCK + WINDOW)
                lhs[rows, 0:WINDOW] = high[:, window]
                lhs[rows, WINDOW : 2 * WINDOW] = low[:, window]
                lhs[rows, 2 * WINDOW : 3 * WINDOW] = high[:, window]
        for pair in range(0, NBASIS, 2):
            bases = range(pair, min(pair + 2, NBASIS))
            cols = slice(pair * BLOCK, (bases[-1] + 1) * BLOCK)
            high, low = split(dot(lhs[0 : COUNT * count, :], col_kernel[:, cols]))
            for block in range(BLKC):
                for visit in range(V):
                    rows = slice((block * V + visit) * count, (block * V + visit + 1) * count)
                    for basis in bases:
                        part = slice((basis - pair) * BLOCK, (basis - pair + 1) * BLOCK)
                        into = slice(fresh, fresh + count), slice(block * BLOCK, (block + 1) * BLOCK)
                        terms_high[visit, basis, into[0], into[1]] = high[rows, part]
                        terms_low[visit, basis, into[0], into[1]] = low[rows, part]

        top = top_row + chunk * CHUNK
        own_rows = (top + lax.broadcasted_iota(jnp.int32, (CHUNK, 1), 0)).astype(jnp.float32)
        row_shift = row_base + row_slope * ((own_rows - (HEIGHT - 1) / 2.0) / HEIGHT)
        row_weight = lanczos(row_shift - row_step)
        position = (top - REACH + lax.broadcasted_iota(jnp.int32, (ROWS_MID, 1), 0)).astype(jnp.float32)
        row_pos = (2.0 * position + 1.0) / HEIGHT - 1.0
        keep = inside(top - REACH, ROWS_MID)
        for visit in range(V):
            constant, by_row, by_column = (
                by_basis(lambda basis: coef_ref[ccd, part, visit, basis]) for part in range(3)
            )
            level = row_kernel * (constant + by_row * row_pos)
            high, low = split(jnp.concatenate([level, row_kernel * by_column], axis=0))
            rows = slice(chunk * CHUNK, chunk * CHUNK + ROWS_IN)
            upper = dot(
                jnp.concatenate([high, low], axis=0), terms_high[visit, :, rows, :].reshape(DEPTH, WIDTH)
            )
            lower = dot(high, terms_low[visit, :, rows, :].reshape(DEPTH, WIDTH))
            both = upper[: 2 * ROWS_MID] + upper[2 * ROWS_MID :] + lower
            matched = both[:ROWS_MID] + both[ROWS_MID:] * col_pos
            mid[visit] = jnp.where(keep, matched, 0.0)

            warped = jnp.zeros((CHUNK, WIDTH), jnp.float32)
            for step in range(STEPS):
                column_of = visit * 8 + step
                warped = warped + row_weight[:, column_of : column_of + 1] * mid[visit, step : step + CHUNK, :]
            total = jnp.zeros((CHUNK, WIDTH), jnp.float32)
            for step in range(STEPS):
                offset = step - REACH
                moved = warped if offset == 0 else pltpu.roll(warped, (-offset) % WIDTH, 1)
                total = total + col_weight[visit][step : step + 1, :] * moved
            rounded = total.astype(jnp.bfloat16)
            for block in range(BLKC):
                stage[turn, visit * BLKC + block] = rounded[:, block * BLOCK : (block + 1) * BLOCK]

        if turn == 0:
            to_plan.wait()
        rows = slice(turn * CHUNK, (turn + 1) * CHUNK)
        for device in range(devices):
            for slot in range(CAP):
                pick = jnp.minimum(jnp.maximum(plan[device, slot], 0), COUNT - 1)
                outbox[device, slot, rows] = stage[turn, pick]
        if turn == 0:
            pl.semaphore_wait(barrier, devices - 1)

            @pl.when(has_next)
            def _():
                to_next().start()

            @pl.when(has_last)
            def _():
                to_last().start()

        for send, turns in enumerate(SENDS):
            if turns[-1] != turn:
                continue
            rows = pl.ds(turns[0] * CHUNK, len(turns) * CHUNK)
            batch = []
            for step in outward(devices):
                target = lax.rem(band + step, devices)
                batch.append(
                    remote(outbox.at[target, :, rows], inbox.at[band, :, rows], send, step)
                )
            batch.append(
                pltpu.make_async_copy(outbox.at[band, :, rows], inbox.at[band, :, rows], own.at[send])
            )
            for copy in batch:
                copy.start()
            batches.append(batch)
        if turn == 0:
            batch = []
            for step in outward(devices):
                batch.append(
                    remote(notes.at[lax.rem(band + step, devices)], table.at[band], sends, step)
                )
            batch.append(pltpu.make_async_copy(notes.at[band], table.at[band], own.at[sends]))
            for copy in batch:
                copy.start()
            note_batch = batch

    for copy in note_batch:
        copy.wait()
    per_tile = BLOCK // (CAP * GROUP)
    cell_tiles, weight_tiles = [], []
    for tile in range(devices // per_tile):
        cell_tile = jnp.zeros((1, BLOCK), jnp.float32)
        weight_tile = jnp.zeros((1, BLOCK), jnp.float32)
        for part in range(per_tile):
            row = table[tile * per_tile + part]
            here = lane // (CAP * GROUP) == part
            cell_tile = jnp.where(here, pltpu.roll(row, part * CAP * GROUP, 1) if part else row, cell_tile)
            shift = (part - 1) * CAP * GROUP % BLOCK
            weight_tile = jnp.where(here, pltpu.roll(row, shift, 1) if shift else row, weight_tile)
        cell_tiles.append(cell_tile)
        weight_tiles.append(weight_tile)
    cell_of = jnp.concatenate(cell_tiles, axis=1)
    weight_of = jnp.concatenate(weight_tiles, axis=1)
    span = devices * CAP * GROUP
    diagonal = lax.broadcasted_iota(jnp.int32, (GROUP, span), 1) % GROUP == lax.broadcasted_iota(
        jnp.int32, (GROUP, span), 0
    )
    mixing = jnp.concatenate(
        [
            jnp.where(diagonal & (cell_of == float(cell)), weight_of, 0.0).astype(jnp.bfloat16)
            for cell in range(CELLS)
        ],
        axis=0,
    )
    sums = dot(mixing, jnp.ones((span, BLOCK), jnp.bfloat16))
    scale = 1.0 / jnp.maximum(sums, 1.0)
    for batch, turns in zip(batches, SENDS):
        for copy in batch:
            copy.wait()
        for turn in turns:
            groups = range(turn * CHUNK, (turn + 1) * CHUNK, GROUP)
            blocks = jnp.concatenate(
                [inbox[:, :, group : group + GROUP, :].reshape(span, BLOCK) for group in groups], axis=1
            )
            result = dot(mixing, blocks)
            for index, group in enumerate(groups):
                part = result[:, index * BLOCK : (index + 1) * BLOCK] * scale
                row = ORDER[turn] * CHUNK + index * GROUP
                for cell in range(CELLS):
                    out_ref[
                        0,
                        cell // PSIDE * BLOCK + row : cell // PSIDE * BLOCK + row + GROUP,
                        cell % PSIDE * BLOCK : (cell % PSIDE + 1) * BLOCK,
                    ] = part[cell * GROUP : (cell + 1) * GROUP]


def shards(
    images, basis_taps, psf_coef, affine, visit_weight, block_patch, block_slot, patch_owner
):
    devices = lax.axis_size("ccd")
    scalars = pl.BlockSpec(memory_space=pltpu.SMEM)
    vector = pl.BlockSpec(memory_space=pltpu.VMEM)
    sends = len(SENDS)
    half = jnp.bfloat16
    size = PSIDE * BLOCK
    return pl.pallas_call(
        functools.partial(band_kernel, devices),
        out_shape=jax.ShapeDtypeStruct((1, size, size), jnp.float32),
        in_specs=[scalars] * 6 + [vector, pl.BlockSpec(memory_space=pl.ANY)],
        out_specs=vector,
        scratch_shapes=[
            pltpu.VMEM((V, EXT, WIDTH), jnp.float32),
            pltpu.VMEM((3 * WINDOW, NBASIS * BLOCK), half),
            pltpu.VMEM((COUNT * ROWS_IN, 3 * WINDOW), half),
            pltpu.VMEM((V, NBASIS, EXT, WIDTH), half),
            pltpu.VMEM((V, NBASIS, EXT, WIDTH), half),
            pltpu.VMEM((V, ROWS_MID, WIDTH), jnp.float32),
            pltpu.VMEM((len(ORDER), COUNT, CHUNK, BLOCK), half),
            pltpu.VMEM((devices, CAP, BLOCK, BLOCK), half),
            pltpu.VMEM((devices, CAP, BLOCK, BLOCK), half),
            pltpu.VMEM((devices, 1, BLOCK), jnp.float32),
            pltpu.VMEM((devices, 1, BLOCK), jnp.float32),
            pltpu.VMEM((devices, BLOCK), jnp.int32),
            pltpu.SMEM((devices, BLOCK), jnp.int32),
            pltpu.SemaphoreType.DMA((sends + 1, devices)),
            pltpu.SemaphoreType.DMA((sends + 1, devices)),
            pltpu.SemaphoreType.DMA((sends + 3,)),
            pltpu.SemaphoreType.DMA((4,)),
        ],
        compiler_params=pltpu.CompilerParams(collective_id=1, has_side_effects=True),
    )(
        basis_taps.transpose(1, 0, 2),
        psf_coef.transpose(1, 3, 0, 2),
        affine.transpose(0, 2, 3, 1),
        block_patch.reshape(-1),
        block_slot,
        patch_owner,
        visit_weight,
        images,
    )


def solution(mesh):
    placed = (
        P(None, ("group", "ccd"), None),
        P(),
        P(None, "group", None, None),
        P(None, "group", None, None),
        P(None, "group"),
        P(("group", "ccd"), None, None),
        P(("group", "ccd"), None),
        P("group"),
    )
    return jax.shard_map(
        shards,
        mesh=mesh,
        in_specs=placed,
        out_specs=P(("group", "ccd"), None, None),
        check_vma=False,
    )
```

```python
import functools
import math

import jax
import jax.numpy as jnp
from jax import lax
from jax.experimental import pallas as pl
from jax.experimental.pallas import tpu as pltpu
from jax.sharding import PartitionSpec as P

V = 4
BLOCK = 128
BLKC = 4
SPLIT = 4
TAPS = 11
NBASIS = 9
PSIDE = 4
CELLS = PSIDE * PSIDE
HALF = TAPS // 2
REACH = 3
RIM = HALF + REACH
CHUNK = 32
CAP = 2
GROUP = 16
EXT = BLOCK + 2 * RIM
ROWS_IN = CHUNK + 2 * RIM
ROWS_MID = CHUNK + 8
WIDTH = BLKC * BLOCK
HEIGHT = SPLIT * BLOCK
LEFT = 16
WINDOW = BLOCK + 2 * LEFT
TILES = -(-3 * WINDOW // BLOCK)
STEPS = 2 * REACH + 1
COUNT = V * BLKC
DEPTH = NBASIS * ROWS_IN
ORDER = (1, 2, 0, 3)
FRESH = ((32, 48), (80, 32), (0, 32), (112, 32))
SENDS = ((0,), (1,), (2, 3))
SINE = [(-1) ** k * math.pi ** (2 * k + 1) / math.factorial(2 * k + 1) for k in range(7)]


def sin_pi(values):
    whole = jnp.floor(values + 0.5)
    rest = values - whole
    odd = whole - 2.0 * jnp.floor(whole * 0.5)
    square = rest * rest
    total = jnp.full(values.shape, SINE[-1], jnp.float32)
    for factor in SINE[-2::-1]:
        total = total * square + factor
    return total * rest * (1.0 - 2.0 * odd)


def finish(product, offset):
    near = jnp.abs(offset) < 1e-4
    square = jnp.where(near, 1.0, offset * offset)
    value = jnp.where(near, 1.0, product * (3.0 / math.pi**2) / square)
    return jnp.where(jnp.abs(offset) < 3.0, value, 0.0)


def lanczos(offset):
    return finish(sin_pi(offset) * sin_pi(offset / 3.0), offset)


def split(values):
    high = values.astype(jnp.bfloat16)
    return high, (values - high.astype(jnp.float32)).astype(jnp.bfloat16)


def dot(left, right):
    return jnp.dot(left, right, preferred_element_type=jnp.float32)


def band_kernel(
    devices,
    taps_in,
    coef_in,
    affine_in,
    patch_in,
    slot_in,
    owner_in,
    weight_in,
    image_ref,
    out_ref,
    taps_ref,
    coef_ref,
    affine_ref,
    patch_ref,
    slot_ref,
    owner_ref,
    weight_ref,
    loads,
    ext,
    col_kernel,
    lhs,
    terms_high,
    terms_low,
    mid,
    stage,
    outbox,
    inbox,
    notes,
    table,
    picks,
    plan,
    sent,
    received,
    own,
    rims,
):
    band = lax.axis_index("ccd")
    barrier = pltpu.get_barrier_semaphore()
    sends = len(SENDS)
    head, tail = FRESH[0][0], FRESH[0][0] + FRESH[0][1]
    pieces = [
        pltpu.make_async_copy(
            image_ref.at[:, pl.ds(low - RIM, high - low)], ext.at[:, pl.ds(low, high - low)], own.at[sends + which]
        )
        for which, (low, high) in ((1, (head, tail)), (3, (RIM, head)), (4, (tail, RIM + BLOCK)))
    ]
    small = [
        pltpu.make_async_copy(source, target, loads.at[which])
        for which, (source, target) in enumerate(
            (
                (taps_in, taps_ref),
                (owner_in, owner_ref),
                (patch_in, patch_ref),
                (slot_in, slot_ref),
                (weight_in, weight_ref),
                (affine_in, affine_ref),
                (coef_in, coef_ref),
            )
        )
    ]
    pieces[0].start()
    for copy in small:
        copy.start()
    for copy in pieces[1:]:
        copy.start()
    for step in range(1, devices):
        pl.semaphore_signal(
            barrier,
            inc=1,
            device_id={"ccd": lax.rem(band + step, devices)},
            device_id_type=pl.DeviceIdType.MESH,
        )
    shifted = band + SPLIT // 2
    ccd = shifted // SPLIT
    top_row = shifted % SPLIT * BLOCK
    region_shift = band * BLOCK - top_row
    region_low = jnp.maximum(0, -region_shift)
    region_high = jnp.minimum(HEIGHT, devices * BLOCK - region_shift)
    lane = lax.broadcasted_iota(jnp.int32, (1, BLOCK), 1)

    def inside(first, count):
        rows = first + lax.broadcasted_iota(jnp.int32, (count, 1), 0)
        return (rows >= region_low) & (rows < region_high)

    pad = jnp.zeros((ROWS_IN, TILES * BLOCK - 3 * WINDOW), jnp.bfloat16)

    def fill(turn):
        fresh, count = FRESH[turn]
        for visit in range(V):
            raw = ext[visit, fresh : fresh + count]
            raw = jnp.where(inside(top_row + fresh - RIM, count), raw, 0.0)
            side = jnp.zeros((count, LEFT), jnp.bfloat16)
            high, low = (jnp.concatenate([side, part, side], axis=1) for part in split(raw))
            for block in range(BLKC):
                rows = slice((block * V + visit) * count, (block * V + visit + 1) * count)
                window = slice(block * BLOCK, block * BLOCK + WINDOW)
                row = jnp.concatenate([high[:, window], low[:, window], high[:, window], pad[:count]], axis=1)
                for tile in range(TILES):
                    lhs[tile, rows] = row[:, tile * BLOCK : (tile + 1) * BLOCK]

    pieces[0].wait()
    fill(0)
    for copy in small:
        copy.wait()

    def make_plan():
        weight_lane = lax.broadcasted_iota(jnp.int32, weight_ref.shape, 1)
        weights = jnp.sum(
            jnp.where(weight_lane == ccd, weight_ref[...].astype(jnp.float32), 0.0), axis=1, keepdims=True
        )
        owners = jnp.full((1, BLOCK), -1, jnp.int32)
        cells = jnp.zeros((1, BLOCK), jnp.float32)
        block_weight = jnp.zeros((1, BLOCK), jnp.float32)
        for block in range(COUNT):
            owners = jnp.where(lane == block, owner_ref[patch_ref[block]], owners)
            cells = jnp.where(lane == block, slot_ref[0, block].astype(jnp.float32), cells)
        for visit in range(V):
            here = jnp.broadcast_to(weights[visit : visit + 1], (1, BLOCK))
            block_weight = jnp.where(lane // BLKC == visit, here, block_weight)
        lanes = lax.broadcasted_iota(jnp.int32, (devices, BLOCK), 1)
        match = owners == lax.broadcasted_iota(jnp.int32, (devices, BLOCK), 0)
        first = jnp.min(jnp.where(match, lanes, BLOCK), axis=1, keepdims=True)
        last = jnp.max(jnp.where(match, lanes, -1), axis=1, keepdims=True)
        is_first, is_last = lanes == first, lanes == last

        def at(chosen, values):
            return jnp.sum(jnp.where(chosen, values, 0.0), axis=1, keepdims=True)

        note = jnp.where(
            lanes < 2 * GROUP,
            jnp.where(lanes < GROUP, at(is_first, cells), at(is_last, cells)),
            jnp.where(
                lanes < 3 * GROUP, at(is_first, block_weight), at(is_last & (last > first), block_weight)
            ),
        )
        picks[...] = jnp.where(lanes == 0, jnp.where(last < 0, 0, first), jnp.maximum(last, 0))
        to_plan = pltpu.make_async_copy(picks, plan, own.at[sends + 2])
        to_plan.start()
        for device in range(devices):
            notes[device] = note[device : device + 1]

        return to_plan

    for basis in range(NBASIS):
        col_kernel[basis, 3 * WINDOW : TILES * BLOCK] = jnp.zeros(
            (TILES * BLOCK - 3 * WINDOW, BLOCK), jnp.bfloat16
        )
    sub = lax.broadcasted_iota(jnp.int32, (8, BLOCK), 0)
    across = lax.broadcasted_iota(jnp.int32, (8, BLOCK), 1)
    edge = LEFT - HALF
    for basis in range(NBASIS):
        taps = jnp.zeros((8, BLOCK), jnp.float32)
        for tap in range(TAPS):
            taps = jnp.where(across == BLOCK - edge - tap, taps_ref[basis, 1, tap], taps)
        taps = pltpu.roll(taps, 0, 1, stride=1, stride_axis=0)
        high = taps.astype(jnp.bfloat16).astype(jnp.float32)
        low = taps - high
        for part, offsets in ((high, (0, WINDOW)), (low, (2 * WINDOW,))):
            rows = []
            for group in range(WINDOW // 8):
                turned = pltpu.roll(part, group * 8 % BLOCK, 1) if group * 8 % BLOCK else part
                tap = group * 8 + sub - edge - across
                rows.append(jnp.where((tap >= 0) & (tap < TAPS), turned, 0.0))
            matrix = jnp.concatenate(rows, axis=0).astype(jnp.bfloat16)
            for offset in offsets:
                col_kernel[basis, offset : offset + WINDOW] = matrix

    wide_lane = lax.broadcasted_iota(jnp.int32, (1, DEPTH), 1)
    starts = [wide_lane >= basis * ROWS_IN for basis in range(NBASIS)]

    def by_basis(value):
        total = jnp.full((1, DEPTH), value(0), jnp.float32)
        for basis in range(1, NBASIS):
            total = jnp.where(starts[basis], value(basis), total)
        return total

    start = jnp.zeros((1, DEPTH), jnp.int32)
    for basis in range(1, NBASIS):
        start = jnp.where(starts[basis], basis * ROWS_IN, start)
    gap = (wide_lane - start) - lax.broadcasted_iota(jnp.int32, (ROWS_MID, DEPTH), 0)
    row_kernel = jnp.zeros(gap.shape, jnp.float32)
    for tap in range(TAPS):
        row_kernel = jnp.where(gap == tap, by_basis(lambda basis: taps_ref[basis, 0, tap]), row_kernel)

    column = lax.broadcasted_iota(jnp.int32, (1, WIDTH), 1).astype(jnp.float32)
    col_pos = (2.0 * column + 1.0) / WIDTH - 1.0
    line = lax.broadcasted_iota(jnp.int32, (8, 1), 0)
    base, slope = jnp.zeros((8, 1), jnp.float32), jnp.zeros((8, 1), jnp.float32)
    for visit in range(V):
        base = jnp.where(line == visit, affine_ref[visit, 1, 0, ccd], base)
        slope = jnp.where(line == visit, affine_ref[visit, 1, 1, ccd], slope)
    col_shift = base + slope * ((column - (WIDTH - 1) / 2.0) / WIDTH)
    sine = sin_pi(col_shift)
    third_sine, third_cosine = sin_pi(col_shift / 3.0), sin_pi(col_shift / 3.0 + 0.5)
    turn_cos, turn_sin = jnp.zeros((8, 1), jnp.float32), jnp.zeros((8, 1), jnp.float32)
    for step in range(STEPS):
        k = step - REACH
        turn_cos = jnp.where(line == step, (-1) ** k * math.cos(math.pi * k / 3), turn_cos)
        turn_sin = jnp.where(line == step, (-1) ** k * math.sin(math.pi * k / 3), turn_sin)
    col_step = lax.broadcasted_iota(jnp.int32, (8, WIDTH), 0) - REACH
    reached = lax.broadcasted_iota(jnp.int32, (8, WIDTH), 1) + col_step
    reached = (reached >= 0) & (reached < WIDTH)
    col_weight = []
    for visit in range(V):
        row = slice(visit, visit + 1)
        product = sine[row] * (third_sine[row] * turn_cos - third_cosine[row] * turn_sin)
        weight = finish(product, col_shift[row] - col_step.astype(jnp.float32))
        col_weight.append(jnp.where(reached, weight, 0.0))

    row_base, row_slope = jnp.zeros((1, BLOCK), jnp.float32), jnp.zeros((1, BLOCK), jnp.float32)
    for visit in range(V):
        row_base = jnp.where(lane // 8 == visit, affine_ref[visit, 0, 0, ccd], row_base)
        row_slope = jnp.where(lane // 8 == visit, affine_ref[visit, 0, 1, ccd], row_slope)
    row_step = (lane % 8 - REACH).astype(jnp.float32)

    def remote(source, target, kind, step):
        return pltpu.make_async_remote_copy(
            src_ref=source,
            dst_ref=target,
            send_sem=sent.at[kind, step],
            recv_sem=received.at[kind, step],
            device_id={"ccd": lax.rem(band + step, devices)},
            device_id_type=pl.DeviceIdType.MESH,
        )

    has_next, has_last = band < devices - 1, band > 0

    def to_next():
        return pltpu.make_async_remote_copy(
            src_ref=image_ref.at[:, pl.ds(BLOCK - RIM, RIM)],
            dst_ref=ext.at[:, pl.ds(0, RIM)],
            send_sem=rims.at[0],
            recv_sem=rims.at[1],
            device_id={"ccd": lax.rem(band + 1, devices)},
            device_id_type=pl.DeviceIdType.MESH,
        )

    def to_last():
        return pltpu.make_async_remote_copy(
            src_ref=image_ref.at[:, pl.ds(0, RIM)],
            dst_ref=ext.at[:, pl.ds(RIM + BLOCK, RIM)],
            send_sem=rims.at[2],
            recv_sem=rims.at[3],
            device_id={"ccd": lax.rem(band + devices - 1, devices)},
            device_id_type=pl.DeviceIdType.MESH,
        )

    batches = []
    for turn, chunk in enumerate(ORDER):
        if chunk == 0:
            @pl.when(has_next)
            def _():
                to_next().wait_send()
                to_last().wait_recv()

            @pl.when(has_last)
            def _():
                to_last().wait_send()
                to_next().wait_recv()

        if turn == 1:
            for copy in pieces[1:]:
                copy.wait()

        fresh, count = FRESH[turn]
        if turn > 0:
            fill(turn)
        for pair in range(0, NBASIS, 2):
            bases = range(pair, min(pair + 2, NBASIS))
            left = jnp.concatenate([lhs[tile, 0 : COUNT * count] for tile in range(TILES)], axis=1)
            right = jnp.concatenate([col_kernel[basis] for basis in bases], axis=1)
            high, low = split(dot(left, right))
            for block in range(BLKC):
                for visit in range(V):
                    rows = slice((block * V + visit) * count, (block * V + visit + 1) * count)
                    for basis in bases:
                        part = slice((basis - pair) * BLOCK, (basis - pair + 1) * BLOCK)
                        terms_high[visit, block, basis, fresh : fresh + count] = high[rows, part]
                        terms_low[visit, block, basis, fresh : fresh + count] = low[rows, part]

        if turn == 0:
            to_plan = make_plan()

        top = top_row + chunk * CHUNK
        own_rows = (top + lax.broadcasted_iota(jnp.int32, (CHUNK, 1), 0)).astype(jnp.float32)
        row_shift = row_base + row_slope * ((own_rows - (HEIGHT - 1) / 2.0) / HEIGHT)
        row_weight = lanczos(row_shift - row_step)
        position = (top - REACH + lax.broadcasted_iota(jnp.int32, (ROWS_MID, 1), 0)).astype(jnp.float32)
        row_pos = (2.0 * position + 1.0) / HEIGHT - 1.0
        keep = inside(top - REACH, ROWS_MID)
        for visit in range(V):
            constant, by_row, by_column = (
                by_basis(lambda basis: coef_ref[ccd, part, visit, basis]) for part in range(3)
            )
            level = row_kernel * (constant + by_row * row_pos)
            high, low = split(jnp.concatenate([level, row_kernel * by_column], axis=0))
            rows = slice(chunk * CHUNK, chunk * CHUNK + ROWS_IN)
            right_high, right_low = (
                jnp.concatenate(
                    [part[visit, block, :, rows, :].reshape(DEPTH, BLOCK) for block in range(BLKC)], axis=1
                )
                for part in (terms_high, terms_low)
            )
            upper = dot(jnp.concatenate([high, low], axis=0), right_high)
            lower = dot(high, right_low)
            both = upper[: 2 * ROWS_MID] + upper[2 * ROWS_MID :] + lower
            matched = both[:ROWS_MID] + both[ROWS_MID:] * col_pos
            mid[visit] = jnp.where(keep, matched, 0.0)

            warped = jnp.zeros((CHUNK, WIDTH), jnp.float32)
            for step in range(STEPS):
                column_of = visit * 8 + step
                warped = warped + row_weight[:, column_of : column_of + 1] * mid[visit, step : step + CHUNK, :]
            total = jnp.zeros((CHUNK, WIDTH), jnp.float32)
            for step in range(STEPS):
                offset = step - REACH
                moved = warped if offset == 0 else pltpu.roll(warped, (-offset) % WIDTH, 1)
                total = total + col_weight[visit][step : step + 1, :] * moved
            rounded = total.astype(jnp.bfloat16)
            for block in range(BLKC):
                stage[turn, visit * BLKC + block] = rounded[:, block * BLOCK : (block + 1) * BLOCK]

        if turn == 0:
            to_plan.wait()
        rows = slice(turn * CHUNK, (turn + 1) * CHUNK)
        for device in range(devices):
            for slot in range(CAP):
                pick = jnp.minimum(jnp.maximum(plan[device, slot], 0), COUNT - 1)
                outbox[device, slot, rows] = stage[turn, pick]
        if turn == 0:
            pl.semaphore_wait(barrier, devices - 1)

            @pl.when(has_next)
            def _():
                to_next().start()

            @pl.when(has_last)
            def _():
                to_last().start()

        for send, turns in enumerate(SENDS):
            if turns[-1] != turn:
                continue
            rows = pl.ds(turns[0] * CHUNK, len(turns) * CHUNK)
            batch = []
            for step in range(1, devices):
                target = lax.rem(band + step, devices)
                batch.append(
                    remote(outbox.at[target, :, rows], inbox.at[band, :, rows], send, step)
                )
            batch.append(
                pltpu.make_async_copy(outbox.at[band, :, rows], inbox.at[band, :, rows], own.at[send])
            )
            for copy in batch:
                copy.start()
            batches.append(batch)
        if turn == 0:
            batch = []
            for step in range(1, devices):
                batch.append(
                    remote(notes.at[lax.rem(band + step, devices)], table.at[band], sends, step)
                )
            batch.append(pltpu.make_async_copy(notes.at[band], table.at[band], own.at[sends]))
            for copy in batch:
                copy.start()
            note_batch = batch

    for copy in note_batch:
        copy.wait()
    per_tile = BLOCK // (CAP * GROUP)
    cell_tiles, weight_tiles = [], []
    for tile in range(devices // per_tile):
        cell_tile = jnp.zeros((1, BLOCK), jnp.float32)
        weight_tile = jnp.zeros((1, BLOCK), jnp.float32)
        for part in range(per_tile):
            row = table[tile * per_tile + part]
            here = lane // (CAP * GROUP) == part
            cell_tile = jnp.where(here, pltpu.roll(row, part * CAP * GROUP, 1) if part else row, cell_tile)
            shift = (part - 1) * CAP * GROUP % BLOCK
            weight_tile = jnp.where(here, pltpu.roll(row, shift, 1) if shift else row, weight_tile)
        cell_tiles.append(cell_tile)
        weight_tiles.append(weight_tile)
    cell_of = jnp.concatenate(cell_tiles, axis=1)
    weight_of = jnp.concatenate(weight_tiles, axis=1)
    span = devices * CAP * GROUP
    diagonal = lax.broadcasted_iota(jnp.int32, (GROUP, span), 1) % GROUP == lax.broadcasted_iota(
        jnp.int32, (GROUP, span), 0
    )
    mixing = jnp.concatenate(
        [
            jnp.where(diagonal & (cell_of == float(cell)), weight_of, 0.0).astype(jnp.bfloat16)
            for cell in range(CELLS)
        ],
        axis=0,
    )
    sums = dot(mixing, jnp.ones((span, BLOCK), jnp.bfloat16))
    scale = 1.0 / jnp.maximum(sums, 1.0)
    for batch, turns in zip(batches, SENDS):
        for copy in batch:
            copy.wait()
        for turn in turns:
            groups = range(turn * CHUNK, (turn + 1) * CHUNK, GROUP)
            blocks = jnp.concatenate(
                [inbox[:, :, group : group + GROUP, :].reshape(span, BLOCK) for group in groups], axis=1
            )
            result = dot(mixing, blocks)
            for index, group in enumerate(groups):
                part = result[:, index * BLOCK : (index + 1) * BLOCK] * scale
                row = ORDER[turn] * CHUNK + index * GROUP
                for cell in range(CELLS):
                    out_ref[
                        0,
                        cell // PSIDE * BLOCK + row : cell // PSIDE * BLOCK + row + GROUP,
                        cell % PSIDE * BLOCK : (cell % PSIDE + 1) * BLOCK,
                    ] = part[cell * GROUP : (cell + 1) * GROUP]


def shards(
    images, basis_taps, psf_coef, affine, visit_weight, block_patch, block_slot, patch_owner
):
    devices = lax.axis_size("ccd")
    small = (
        basis_taps.transpose(1, 0, 2),
        psf_coef.transpose(1, 3, 0, 2),
        affine.transpose(0, 2, 3, 1),
        block_patch.reshape(-1),
        block_slot,
        patch_owner,
        visit_weight,
    )
    vector = pl.BlockSpec(memory_space=pltpu.VMEM)
    sends = len(SENDS)
    half = jnp.bfloat16
    size = PSIDE * BLOCK
    return pl.pallas_call(
        functools.partial(band_kernel, devices),
        out_shape=jax.ShapeDtypeStruct((1, size, size), jnp.float32),
        in_specs=[pl.BlockSpec(memory_space=pltpu.HBM)] * (len(small) + 1),
        out_specs=vector,
        scratch_shapes=[pltpu.SMEM(array.shape, array.dtype) for array in small[:-1]]
        + [
            pltpu.VMEM(visit_weight.shape, half),
            pltpu.SemaphoreType.DMA((len(small),)),
            pltpu.VMEM((V, EXT, WIDTH), jnp.float32),
            pltpu.VMEM((NBASIS, TILES * BLOCK, BLOCK), half),
            pltpu.VMEM((TILES, COUNT * ROWS_IN, BLOCK), half),
            pltpu.VMEM((V, BLKC, NBASIS, EXT, BLOCK), half),
            pltpu.VMEM((V, BLKC, NBASIS, EXT, BLOCK), half),
            pltpu.VMEM((V, ROWS_MID, WIDTH), jnp.float32),
            pltpu.VMEM((len(ORDER), COUNT, CHUNK, BLOCK), half),
            pltpu.VMEM((devices, CAP, BLOCK, BLOCK), half),
            pltpu.VMEM((devices, CAP, BLOCK, BLOCK), half),
            pltpu.VMEM((devices, 1, BLOCK), jnp.float32),
            pltpu.VMEM((devices, 1, BLOCK), jnp.float32),
            pltpu.VMEM((devices, BLOCK), jnp.int32),
            pltpu.SMEM((devices, BLOCK), jnp.int32),
            pltpu.SemaphoreType.DMA((sends + 1, devices)),
            pltpu.SemaphoreType.DMA((sends + 1, devices)),
            pltpu.SemaphoreType.DMA((sends + 5,)),
            pltpu.SemaphoreType.DMA((4,)),
        ],
        compiler_params=pltpu.CompilerParams(collective_id=1, has_side_effects=True, vmem_limit_bytes=40 << 20),
    )(*(pltpu.with_memory_space_constraint(array, pltpu.HBM) for array in (*small, images)))


def solution(mesh):
    placed = (
        P(None, ("group", "ccd"), None),
        P(),
        P(None, "group", None, None),
        P(None, "group", None, None),
        P(None, "group"),
        P(("group", "ccd"), None, None),
        P(("group", "ccd"), None),
        P("group"),
    )
    return jax.shard_map(
        shards,
        mesh=mesh,
        in_specs=placed,
        out_specs=P(("group", "ccd"), None, None),
        check_vma=False,
    )
```

```python
import functools
import math

import jax
import jax.numpy as jnp
from jax import lax
from jax.experimental import pallas as pl
from jax.experimental.pallas import tpu as pltpu
from jax.sharding import PartitionSpec as P

V = 4
BLOCK = 128
BLKC = 4
SPLIT = 4
TAPS = 11
NBASIS = 9
PSIDE = 4
CELLS = PSIDE * PSIDE
HALF = TAPS // 2
REACH = 3
RIM = HALF + REACH
CAP = 2
GROUP = 16
EXT = BLOCK + 2 * RIM
WIDTH = BLKC * BLOCK
HEIGHT = SPLIT * BLOCK
LEFT = 16
WINDOW = BLOCK + 2 * LEFT
TILES = -(-3 * WINDOW // BLOCK)
STEPS = 2 * REACH + 1
COUNT = V * BLKC
TURNS = ((48, 16, 48, 32), (64, 48, 80, 48), (0, 48, 0, 48), (112, 16, 128, 16))
OFFSETS = tuple(sum(turn[1] for turn in TURNS[:index]) for index in range(len(TURNS)))
MOST = max(turn[1] for turn in TURNS)
FRESH = tuple(turn[2:] for turn in TURNS)
LINES = max(turn[3] for turn in TURNS)
SENDS = ((0,), (1,), (2, 3))
SINE = [(-1) ** k * math.pi ** (2 * k + 1) / math.factorial(2 * k + 1) for k in range(7)]


def sin_pi(values):
    whole = jnp.floor(values + 0.5)
    rest = values - whole
    odd = whole - 2.0 * jnp.floor(whole * 0.5)
    square = rest * rest
    total = jnp.full(values.shape, SINE[-1], jnp.float32)
    for factor in SINE[-2::-1]:
        total = total * square + factor
    return total * rest * (1.0 - 2.0 * odd)


def finish(product, offset):
    near = jnp.abs(offset) < 1e-4
    square = jnp.where(near, 1.0, offset * offset)
    value = jnp.where(near, 1.0, product * (3.0 / math.pi**2) / square)
    return jnp.where(jnp.abs(offset) < 3.0, value, 0.0)


def lanczos(offset):
    return finish(sin_pi(offset) * sin_pi(offset / 3.0), offset)


def split(values):
    high = values.astype(jnp.bfloat16)
    return high, (values - high.astype(jnp.float32)).astype(jnp.bfloat16)


def dot(left, right):
    return jnp.dot(left, right, preferred_element_type=jnp.float32)


def band_kernel(
    devices,
    taps_in,
    coef_in,
    affine_in,
    patch_in,
    slot_in,
    owner_in,
    weight_in,
    image_ref,
    out_ref,
    taps_ref,
    coef_ref,
    affine_ref,
    patch_ref,
    slot_ref,
    owner_ref,
    weight_ref,
    loads,
    ext,
    col_kernel,
    lhs,
    terms_high,
    terms_low,
    mid,
    stage,
    outbox,
    inbox,
    notes,
    table,
    picks,
    plan,
    sent,
    received,
    own,
    rims,
):
    band = lax.axis_index("ccd")
    barrier = pltpu.get_barrier_semaphore()
    sends = len(SENDS)
    head, tail = FRESH[0][0], FRESH[0][0] + FRESH[0][1]
    pieces = [
        pltpu.make_async_copy(
            image_ref.at[:, pl.ds(low - RIM, high - low)], ext.at[:, pl.ds(low, high - low)], own.at[sends + which]
        )
        for which, (low, high) in ((1, (head, tail)), (3, (RIM, head)), (4, (tail, RIM + BLOCK)))
    ]
    small = [
        pltpu.make_async_copy(source, target, loads.at[which])
        for which, (source, target) in enumerate(
            (
                (taps_in, taps_ref),
                (owner_in, owner_ref),
                (patch_in, patch_ref),
                (slot_in, slot_ref),
                (weight_in, weight_ref),
                (affine_in, affine_ref),
                (coef_in, coef_ref),
            )
        )
    ]
    pieces[0].start()
    for copy in small:
        copy.start()
    for copy in pieces[1:]:
        copy.start()
    for step in range(1, devices):
        pl.semaphore_signal(
            barrier,
            inc=1,
            device_id={"ccd": lax.rem(band + step, devices)},
            device_id_type=pl.DeviceIdType.MESH,
        )
    shifted = band + SPLIT // 2
    ccd = shifted // SPLIT
    top_row = shifted % SPLIT * BLOCK
    region_shift = band * BLOCK - top_row
    region_low = jnp.maximum(0, -region_shift)
    region_high = jnp.minimum(HEIGHT, devices * BLOCK - region_shift)
    lane = lax.broadcasted_iota(jnp.int32, (1, BLOCK), 1)

    def inside(first, count):
        rows = first + lax.broadcasted_iota(jnp.int32, (count, 1), 0)
        return (rows >= region_low) & (rows < region_high)

    pad = jnp.zeros((LINES, TILES * BLOCK - 3 * WINDOW), jnp.bfloat16)

    def fill(turn):
        fresh, count = FRESH[turn]
        for visit in range(V):
            raw = ext[visit, fresh : fresh + count]
            raw = jnp.where(inside(top_row + fresh - RIM, count), raw, 0.0)
            side = jnp.zeros((count, LEFT), jnp.bfloat16)
            high, low = (jnp.concatenate([side, part, side], axis=1) for part in split(raw))
            for block in range(BLKC):
                rows = slice((block * V + visit) * count, (block * V + visit + 1) * count)
                window = slice(block * BLOCK, block * BLOCK + WINDOW)
                row = jnp.concatenate([high[:, window], low[:, window], high[:, window], pad[:count]], axis=1)
                for tile in range(TILES):
                    lhs[tile, rows] = row[:, tile * BLOCK : (tile + 1) * BLOCK]

    pieces[0].wait()
    fill(0)
    for copy in small:
        copy.wait()

    def make_plan():
        weight_lane = lax.broadcasted_iota(jnp.int32, weight_ref.shape, 1)
        weights = jnp.sum(
            jnp.where(weight_lane == ccd, weight_ref[...].astype(jnp.float32), 0.0), axis=1, keepdims=True
        )
        owners = jnp.full((1, BLOCK), -1, jnp.int32)
        cells = jnp.zeros((1, BLOCK), jnp.float32)
        block_weight = jnp.zeros((1, BLOCK), jnp.float32)
        for block in range(COUNT):
            owners = jnp.where(lane == block, owner_ref[patch_ref[block]], owners)
            cells = jnp.where(lane == block, slot_ref[0, block].astype(jnp.float32), cells)
        for visit in range(V):
            here = jnp.broadcast_to(weights[visit : visit + 1], (1, BLOCK))
            block_weight = jnp.where(lane // BLKC == visit, here, block_weight)
        lanes = lax.broadcasted_iota(jnp.int32, (devices, BLOCK), 1)
        match = owners == lax.broadcasted_iota(jnp.int32, (devices, BLOCK), 0)
        first = jnp.min(jnp.where(match, lanes, BLOCK), axis=1, keepdims=True)
        last = jnp.max(jnp.where(match, lanes, -1), axis=1, keepdims=True)
        is_first, is_last = lanes == first, lanes == last

        def at(chosen, values):
            return jnp.sum(jnp.where(chosen, values, 0.0), axis=1, keepdims=True)

        note = jnp.where(
            lanes < 2 * GROUP,
            jnp.where(lanes < GROUP, at(is_first, cells), at(is_last, cells)),
            jnp.where(
                lanes < 3 * GROUP, at(is_first, block_weight), at(is_last & (last > first), block_weight)
            ),
        )
        picks[...] = jnp.where(lanes == 0, jnp.where(last < 0, 0, first), jnp.maximum(last, 0))
        to_plan = pltpu.make_async_copy(picks, plan, own.at[sends + 2])
        to_plan.start()
        for device in range(devices):
            notes[device] = note[device : device + 1]

        return to_plan

    for basis in range(NBASIS):
        col_kernel[basis, 3 * WINDOW : TILES * BLOCK] = jnp.zeros(
            (TILES * BLOCK - 3 * WINDOW, BLOCK), jnp.bfloat16
        )
    sub = lax.broadcasted_iota(jnp.int32, (8, BLOCK), 0)
    across = lax.broadcasted_iota(jnp.int32, (8, BLOCK), 1)
    edge = LEFT - HALF
    for basis in range(NBASIS):
        taps = jnp.zeros((8, BLOCK), jnp.float32)
        for tap in range(TAPS):
            taps = jnp.where(across == BLOCK - edge - tap, taps_ref[basis, 1, tap], taps)
        taps = pltpu.roll(taps, 0, 1, stride=1, stride_axis=0)
        high = taps.astype(jnp.bfloat16).astype(jnp.float32)
        low = taps - high
        for part, offsets in ((high, (0, WINDOW)), (low, (2 * WINDOW,))):
            rows = []
            for group in range(WINDOW // 8):
                top = group * 8
                if top + 7 < edge or top - edge - TAPS + 1 > BLOCK - 1:
                    rows.append(jnp.zeros((8, BLOCK), jnp.float32))
                    continue
                turned = pltpu.roll(part, top % BLOCK, 1) if top % BLOCK else part
                if top - edge - TAPS + 1 < 0 or top + 7 - edge > BLOCK - 1:
                    tap = top + sub - edge - across
                    turned = jnp.where((tap >= 0) & (tap < TAPS), turned, 0.0)
                rows.append(turned)
            matrix = jnp.concatenate(rows, axis=0).astype(jnp.bfloat16)
            for offset in offsets:
                col_kernel[basis, offset : offset + WINDOW] = matrix

    def row_band(count):
        rows_in, rows_mid = count + 2 * RIM, count + 8
        depth = NBASIS * rows_in
        wide_lane = lax.broadcasted_iota(jnp.int32, (1, depth), 1)
        starts = [wide_lane >= basis * rows_in for basis in range(NBASIS)]

        def by_basis(value):
            total = jnp.full((1, depth), value(0), jnp.float32)
            for basis in range(1, NBASIS):
                total = jnp.where(starts[basis], value(basis), total)
            return total

        start = jnp.zeros((1, depth), jnp.int32)
        for basis in range(1, NBASIS):
            start = jnp.where(starts[basis], basis * rows_in, start)
        gap = (wide_lane - start) - lax.broadcasted_iota(jnp.int32, (rows_mid, depth), 0)
        row_kernel = jnp.zeros(gap.shape, jnp.float32)
        for tap in range(TAPS):
            row_kernel = jnp.where(gap == tap, by_basis(lambda basis: taps_ref[basis, 0, tap]), row_kernel)
        return row_kernel, by_basis

    bands = {TURNS[0][1]: row_band(TURNS[0][1])}

    column = lax.broadcasted_iota(jnp.int32, (1, WIDTH), 1).astype(jnp.float32)
    col_pos = (2.0 * column + 1.0) / WIDTH - 1.0
    line = lax.broadcasted_iota(jnp.int32, (8, 1), 0)
    base, slope = jnp.zeros((8, 1), jnp.float32), jnp.zeros((8, 1), jnp.float32)
    for visit in range(V):
        base = jnp.where(line == visit, affine_ref[visit, 1, 0, ccd], base)
        slope = jnp.where(line == visit, affine_ref[visit, 1, 1, ccd], slope)
    col_shift = base + slope * ((column - (WIDTH - 1) / 2.0) / WIDTH)
    sine = sin_pi(col_shift)
    third_sine, third_cosine = sin_pi(col_shift / 3.0), sin_pi(col_shift / 3.0 + 0.5)
    turn_cos, turn_sin = jnp.zeros((8, 1), jnp.float32), jnp.zeros((8, 1), jnp.float32)
    for step in range(STEPS):
        k = step - REACH
        turn_cos = jnp.where(line == step, (-1) ** k * math.cos(math.pi * k / 3), turn_cos)
        turn_sin = jnp.where(line == step, (-1) ** k * math.sin(math.pi * k / 3), turn_sin)
    col_step = lax.broadcasted_iota(jnp.int32, (8, WIDTH), 0) - REACH
    reached = lax.broadcasted_iota(jnp.int32, (8, WIDTH), 1) + col_step
    reached = (reached >= 0) & (reached < WIDTH)
    col_weight = []
    for visit in range(V):
        row = slice(visit, visit + 1)
        product = sine[row] * (third_sine[row] * turn_cos - third_cosine[row] * turn_sin)
        weight = finish(product, col_shift[row] - col_step.astype(jnp.float32))
        col_weight.append(jnp.where(reached, weight, 0.0))

    row_base, row_slope = jnp.zeros((1, BLOCK), jnp.float32), jnp.zeros((1, BLOCK), jnp.float32)
    for visit in range(V):
        row_base = jnp.where(lane // 8 == visit, affine_ref[visit, 0, 0, ccd], row_base)
        row_slope = jnp.where(lane // 8 == visit, affine_ref[visit, 0, 1, ccd], row_slope)
    row_step = (lane % 8 - REACH).astype(jnp.float32)

    def remote(source, target, kind, step):
        return pltpu.make_async_remote_copy(
            src_ref=source,
            dst_ref=target,
            send_sem=sent.at[kind, step],
            recv_sem=received.at[kind, step],
            device_id={"ccd": lax.rem(band + step, devices)},
            device_id_type=pl.DeviceIdType.MESH,
        )

    has_next, has_last = band < devices - 1, band > 0

    def to_next():
        return pltpu.make_async_remote_copy(
            src_ref=image_ref.at[:, pl.ds(BLOCK - RIM, RIM)],
            dst_ref=ext.at[:, pl.ds(0, RIM)],
            send_sem=rims.at[0],
            recv_sem=rims.at[1],
            device_id={"ccd": lax.rem(band + 1, devices)},
            device_id_type=pl.DeviceIdType.MESH,
        )

    def to_last():
        return pltpu.make_async_remote_copy(
            src_ref=image_ref.at[:, pl.ds(0, RIM)],
            dst_ref=ext.at[:, pl.ds(RIM + BLOCK, RIM)],
            send_sem=rims.at[2],
            recv_sem=rims.at[3],
            device_id={"ccd": lax.rem(band + devices - 1, devices)},
            device_id_type=pl.DeviceIdType.MESH,
        )

    batches = []
    for turn, (begin, size, _, _) in enumerate(TURNS):
        if turn == 2:
            @pl.when(has_next)
            def _():
                to_next().wait_send()
                to_last().wait_recv()

            @pl.when(has_last)
            def _():
                to_last().wait_send()
                to_next().wait_recv()

        if turn == 1:
            for copy in pieces[1:]:
                copy.wait()

        fresh, count = FRESH[turn]
        if turn > 0:
            fill(turn)
        for pair in range(0, NBASIS, 2):
            bases = range(pair, min(pair + 2, NBASIS))
            left = jnp.concatenate([lhs[tile, 0 : COUNT * count] for tile in range(TILES)], axis=1)
            right = jnp.concatenate([col_kernel[basis] for basis in bases], axis=1)
            high, low = split(dot(left, right))
            for block in range(BLKC):
                for visit in range(V):
                    rows = slice((block * V + visit) * count, (block * V + visit + 1) * count)
                    for basis in bases:
                        part = slice((basis - pair) * BLOCK, (basis - pair + 1) * BLOCK)
                        terms_high[visit, block, basis, fresh : fresh + count] = high[rows, part]
                        terms_low[visit, block, basis, fresh : fresh + count] = low[rows, part]

        if turn == 0:
            to_plan = make_plan()

        if size not in bands:
            bands[size] = row_band(size)
        row_kernel, by_basis = bands[size]
        rows_in, rows_mid = size + 2 * RIM, size + 8
        depth = NBASIS * rows_in
        top = top_row + begin
        own_rows = (top + lax.broadcasted_iota(jnp.int32, (size, 1), 0)).astype(jnp.float32)
        row_shift = row_base + row_slope * ((own_rows - (HEIGHT - 1) / 2.0) / HEIGHT)
        row_weight = lanczos(row_shift - row_step)
        position = (top - REACH + lax.broadcasted_iota(jnp.int32, (rows_mid, 1), 0)).astype(jnp.float32)
        row_pos = (2.0 * position + 1.0) / HEIGHT - 1.0
        keep = inside(top - REACH, rows_mid)
        for visit in range(V):
            constant, by_row, by_column = (
                by_basis(lambda basis: coef_ref[ccd, part, visit, basis]) for part in range(3)
            )
            level = row_kernel * (constant + by_row * row_pos)
            high, low = split(jnp.concatenate([level, row_kernel * by_column], axis=0))
            rows = slice(begin, begin + rows_in)
            right_high, right_low = (
                jnp.concatenate(
                    [part[visit, block, :, rows, :].reshape(depth, BLOCK) for block in range(BLKC)], axis=1
                )
                for part in (terms_high, terms_low)
            )
            upper = dot(jnp.concatenate([high, low], axis=0), right_high)
            lower = dot(high, right_low)
            both = upper[: 2 * rows_mid] + upper[2 * rows_mid :] + lower
            matched = both[:rows_mid] + both[rows_mid:] * col_pos
            mid[visit, 0:rows_mid] = jnp.where(keep, matched, 0.0)

            warped = jnp.zeros((size, WIDTH), jnp.float32)
            for step in range(STEPS):
                column_of = visit * 8 + step
                warped = warped + row_weight[:, column_of : column_of + 1] * mid[visit, step : step + size, :]
            total = jnp.zeros((size, WIDTH), jnp.float32)
            for step in range(STEPS):
                offset = step - REACH
                moved = warped if offset == 0 else pltpu.roll(warped, (-offset) % WIDTH, 1)
                total = total + col_weight[visit][step : step + 1, :] * moved
            rounded = total.astype(jnp.bfloat16)
            for block in range(BLKC):
                stage[turn, visit * BLKC + block, 0:size] = rounded[:, block * BLOCK : (block + 1) * BLOCK]

        if turn == 0:
            to_plan.wait()
        rows = slice(OFFSETS[turn], OFFSETS[turn] + size)
        for device in range(devices):
            for slot in range(CAP):
                pick = jnp.minimum(jnp.maximum(plan[device, slot], 0), COUNT - 1)
                outbox[device, slot, rows] = stage[turn, pick, 0:size]
        if turn == 0:
            pl.semaphore_wait(barrier, devices - 1)

            @pl.when(has_next)
            def _():
                to_next().start()

            @pl.when(has_last)
            def _():
                to_last().start()

        for send, turns in enumerate(SENDS):
            if turns[-1] != turn:
                continue
            rows = pl.ds(OFFSETS[turns[0]], sum(TURNS[each][1] for each in turns))
            batch = []
            for step in range(1, devices):
                target = lax.rem(band + step, devices)
                batch.append(
                    remote(outbox.at[target, :, rows], inbox.at[band, :, rows], send, step)
                )
            batch.append(
                pltpu.make_async_copy(outbox.at[band, :, rows], inbox.at[band, :, rows], own.at[send])
            )
            for copy in batch:
                copy.start()
            batches.append(batch)
        if turn == 0:
            batch = []
            for step in range(1, devices):
                batch.append(
                    remote(notes.at[lax.rem(band + step, devices)], table.at[band], sends, step)
                )
            batch.append(pltpu.make_async_copy(notes.at[band], table.at[band], own.at[sends]))
            for copy in batch:
                copy.start()
            note_batch = batch

    for copy in note_batch:
        copy.wait()
    per_tile = BLOCK // (CAP * GROUP)
    cell_tiles, weight_tiles = [], []
    for tile in range(devices // per_tile):
        cell_tile = jnp.zeros((1, BLOCK), jnp.float32)
        weight_tile = jnp.zeros((1, BLOCK), jnp.float32)
        for part in range(per_tile):
            row = table[tile * per_tile + part]
            here = lane // (CAP * GROUP) == part
            cell_tile = jnp.where(here, pltpu.roll(row, part * CAP * GROUP, 1) if part else row, cell_tile)
            shift = (part - 1) * CAP * GROUP % BLOCK
            weight_tile = jnp.where(here, pltpu.roll(row, shift, 1) if shift else row, weight_tile)
        cell_tiles.append(cell_tile)
        weight_tiles.append(weight_tile)
    cell_of = jnp.concatenate(cell_tiles, axis=1)
    weight_of = jnp.concatenate(weight_tiles, axis=1)
    span = devices * CAP * GROUP
    diagonal = lax.broadcasted_iota(jnp.int32, (GROUP, span), 1) % GROUP == lax.broadcasted_iota(
        jnp.int32, (GROUP, span), 0
    )
    mixing = jnp.concatenate(
        [
            jnp.where(diagonal & (cell_of == float(cell)), weight_of, 0.0).astype(jnp.bfloat16)
            for cell in range(CELLS)
        ],
        axis=0,
    )
    sums = dot(mixing, jnp.ones((span, BLOCK), jnp.bfloat16))
    scale = 1.0 / jnp.maximum(sums, 1.0)
    for batch, turns in zip(batches, SENDS):
        for copy in batch:
            copy.wait()
        for turn in turns:
            groups = range(OFFSETS[turn], OFFSETS[turn] + TURNS[turn][1], GROUP)
            blocks = jnp.concatenate(
                [inbox[:, :, group : group + GROUP, :].reshape(span, BLOCK) for group in groups], axis=1
            )
            result = dot(mixing, blocks)
            for index, group in enumerate(groups):
                part = result[:, index * BLOCK : (index + 1) * BLOCK] * scale
                row = TURNS[turn][0] + index * GROUP
                for cell in range(CELLS):
                    out_ref[
                        0,
                        cell // PSIDE * BLOCK + row : cell // PSIDE * BLOCK + row + GROUP,
                        cell % PSIDE * BLOCK : (cell % PSIDE + 1) * BLOCK,
                    ] = part[cell * GROUP : (cell + 1) * GROUP]


def shards(
    images, basis_taps, psf_coef, affine, visit_weight, block_patch, block_slot, patch_owner
):
    devices = lax.axis_size("ccd")
    small = (
        basis_taps.transpose(1, 0, 2),
        psf_coef.transpose(1, 3, 0, 2),
        affine.transpose(0, 2, 3, 1),
        block_patch.reshape(-1),
        block_slot,
        patch_owner,
        visit_weight,
    )
    vector = pl.BlockSpec(memory_space=pltpu.VMEM)
    sends = len(SENDS)
    half = jnp.bfloat16
    size = PSIDE * BLOCK
    return pl.pallas_call(
        functools.partial(band_kernel, devices),
        out_shape=jax.ShapeDtypeStruct((1, size, size), jnp.float32),
        in_specs=[pl.BlockSpec(memory_space=pltpu.HBM)] * (len(small) + 1),
        out_specs=vector,
        scratch_shapes=[pltpu.SMEM(array.shape, array.dtype) for array in small[:-1]]
        + [
            pltpu.VMEM(visit_weight.shape, half),
            pltpu.SemaphoreType.DMA((len(small),)),
            pltpu.VMEM((V, EXT, WIDTH), jnp.float32),
            pltpu.VMEM((NBASIS, TILES * BLOCK, BLOCK), half),
            pltpu.VMEM((TILES, COUNT * LINES, BLOCK), half),
            pltpu.VMEM((V, BLKC, NBASIS, EXT, BLOCK), half),
            pltpu.VMEM((V, BLKC, NBASIS, EXT, BLOCK), half),
            pltpu.VMEM((V, MOST + 8, WIDTH), jnp.float32),
            pltpu.VMEM((len(TURNS), COUNT, MOST, BLOCK), half),
            pltpu.VMEM((devices, CAP, BLOCK, BLOCK), half),
            pltpu.VMEM((devices, CAP, BLOCK, BLOCK), half),
            pltpu.VMEM((devices, 1, BLOCK), jnp.float32),
            pltpu.VMEM((devices, 1, BLOCK), jnp.float32),
            pltpu.VMEM((devices, BLOCK), jnp.int32),
            pltpu.SMEM((devices, BLOCK), jnp.int32),
            pltpu.SemaphoreType.DMA((sends + 1, devices)),
            pltpu.SemaphoreType.DMA((sends + 1, devices)),
            pltpu.SemaphoreType.DMA((sends + 5,)),
            pltpu.SemaphoreType.DMA((4,)),
        ],
        compiler_params=pltpu.CompilerParams(collective_id=1, has_side_effects=True, vmem_limit_bytes=40 << 20),
    )(*(pltpu.with_memory_space_constraint(array, pltpu.HBM) for array in (*small, images)))


def solution(mesh):
    placed = (
        P(None, ("group", "ccd"), None),
        P(),
        P(None, "group", None, None),
        P(None, "group", None, None),
        P(None, "group"),
        P(("group", "ccd"), None, None),
        P(("group", "ccd"), None),
        P("group"),
    )
    return jax.shard_map(
        shards,
        mesh=mesh,
        in_specs=placed,
        out_specs=P(("group", "ccd"), None, None),
        check_vma=False,
    )
```
